128 devices in a mesh: row: 8 (over z, core), col: 16 (over x, y).
Axes of the slice: x: 4, y: 4, z: 4, core: 2. Of those that a mesh axis runs over, the one named last changes fastest.
Arguments:
- colloc_points: float32 [3, 61440], P(None, 'row'), may hold values from -1 to 1, as said below
- sources: float32 [4, 2048], P(None, 'col'), may hold values from -1 to 1, as said below
- counts: int32 [480, 16], P('row', 'col'), may hold values from 2 to 16, as said below
- row_element: int32 [61440], P('row'), may hold values from 0 to 61439, as said below
- pivots: int32 [128], replicated, may hold values from 0 to 61439, as said below
Outputs:
- factored: float32 [61440, 2048], P('row', 'col')
- u_rows: float32 [128, 2048], P(None, 'col')
The draws below stay inside these ranges and needn't reach their ends.
Inputs may be any that keep to these rules, and one draw needn't show every extreme that they name: `counts`: every tile uses 2 to 16 quadrature points, and some tile uses 16. `row_element`: a permutation of the 61440 elements. pivots[k] is the row r with row_element[r] == k. `colloc_points`: first two coordinates between 0 and 1, third between -0.1 and 0.1. `sources`: centres as for the collocation points; core radii between 0.05 and 0.15.
All inputs are finite; a program needn't handle non-finite values.
Results may differ from the reference program's by a relative error of at most 0.0003.
Values sent between devices are 32-bit elements; how exact they have to be, the bound alone decides.
No kernel may reach another device: no remote copies, remote signals or barrier semaphores. Data moves between devices by JAX's collectives and lax.ppermute only.
A program may use at most 64 MiB of HBM per device.

```python
import jax
import jax.numpy as jnp
from jax import lax

MATRIX_ORDER = 61440
TILE_SIZE = 128
QUAD_MAX = 16
TILE_COLS_DEV = 1
TILE_ROWS_DEV = 60
ROW_TILES = 480
COL_TILES = 16
WINDOW_COLS = 2048


def element_order(key):
    return jax.random.permutation(jax.random.fold_in(key, 11), MATRIX_ORDER).astype(jnp.int32)


def draw_row_element(key, part):
    return element_order(key)


def draw_pivots(key, part):
    ordering = element_order(key)
    return jnp.argsort(ordering, stable=True)[:TILE_SIZE].astype(jnp.int32)


def surface_points(key, amount):
    subkeys = jax.random.split(jax.random.fold_in(key, 23), 2)
    plane = jax.random.uniform(subkeys[0], (2, amount), jnp.float32)
    height = jax.random.uniform(subkeys[1], (1, amount), jnp.float32, -0.1, 0.1)
    return jnp.concatenate([plane, height], 0)


def draw_colloc_points(key, part):
    return surface_points(key, MATRIX_ORDER)


def draw_sources(key, part):
    centres = surface_points(jax.random.fold_in(key, 5), WINDOW_COLS)
    logs = jax.random.uniform(jax.random.fold_in(key, 7), (1, WINDOW_COLS), jnp.float32, jnp.log(0.05), jnp.log(0.15))
    sizes = jnp.exp(logs)
    return jnp.concatenate([centres, sizes], 0)


def draw_counts(key, part):
    subkeys = jax.random.split(jax.random.fold_in(key, 31), 4)
    drawn = jax.random.randint(subkeys[0], (ROW_TILES, COL_TILES), 2, 7)
    near_tip = jax.random.randint(subkeys[1], (ROW_TILES, COL_TILES), 12, QUAD_MAX + 1)
    band_row = jax.random.randint(subkeys[2], (), 0, ROW_TILES // TILE_ROWS_DEV)
    band_col = jax.random.randint(subkeys[3], (), 0, COL_TILES // TILE_COLS_DEV)
    rows_group = jnp.arange(ROW_TILES)[:, None] // TILE_ROWS_DEV
    cols_group = jnp.arange(COL_TILES)[None, :] // TILE_COLS_DEV
    in_region = (rows_group == band_row) & (cols_group == band_col)
    tiles = jnp.where(in_region, near_tip, drawn)
    tiles = tiles.at[band_row * TILE_ROWS_DEV, band_col * TILE_COLS_DEV].set(QUAD_MAX)
    return tiles.astype(jnp.int32)


def setup_inputs(seed: int = 0) -> dict:
    splits = jax.random.split(jax.random.key(seed), 6)
    return {
        "colloc_points": draw_colloc_points(jax.random.fold_in(splits[5], 71), 0),
        "sources": draw_sources(jax.random.fold_in(splits[5], 71), 0),
        "counts": draw_counts(jax.random.fold_in(splits[5], 71), 0),
        "row_element": draw_row_element(jax.random.fold_in(splits[5], 71), 0),
        "pivots": draw_pivots(jax.random.fold_in(splits[5], 71), 0),
    }


jump_factor = 4.0
disc_radius = 4.0

def quad_offsets():
    numbers = jnp.arange(QUAD_MAX).astype(jnp.float32)
    radius = disc_radius * jnp.sqrt((numbers + 0.5) / QUAD_MAX)
    angles = 2.39996323 * numbers
    return (radius * jnp.cos(angles), radius * jnp.sin(angles))

def kelvin_entry(point_x, point_y, point_z, source_x, source_y, source_z, source_size):
    delta_x = point_x - source_x
    delta_y = point_y - source_y
    delta_z = point_z - source_z
    rho_sq = delta_x * delta_x + delta_y * delta_y + delta_z * delta_z + source_size * source_size
    return (2.0 + delta_z * delta_z / rho_sq) * lax.rsqrt(rho_sq)

def lower_unit_inverse(lower_unit):
    side = lower_unit.shape[0]
    positions = jnp.arange(side)
    strict = jnp.tril(lower_unit, -1)

    def step(index, inverse):
        unit_row = (positions == index).astype(inverse.dtype)
        strict_row = lax.dynamic_index_in_dim(strict, index, 0, keepdims=False)
        new_row = unit_row - jnp.dot(strict_row, inverse, precision=lax.Precision.HIGHEST)
        return lax.dynamic_update_index_in_dim(inverse, new_row, index, 0)
    return lax.fori_loop(0, side, step, jnp.zeros_like(lower_unit))

def upper_inverse(upper_part):
    side = upper_part.shape[0]
    positions = jnp.arange(side)
    strict = jnp.triu(upper_part, 1)

    def step(count, inverse):
        index = side - 1 - count
        unit_row = (positions == index).astype(inverse.dtype)
        strict_row = lax.dynamic_index_in_dim(strict, index, 0, keepdims=False)
        full_row = lax.dynamic_index_in_dim(upper_part, index, 0, keepdims=False)
        pivot_value = lax.dynamic_index_in_dim(full_row, index, 0, keepdims=False)
        new_row = (unit_row - jnp.dot(strict_row, inverse, precision=lax.Precision.HIGHEST)) / pivot_value
        return lax.dynamic_update_index_in_dim(inverse, new_row, index, 0)
    return lax.fori_loop(0, side, step, jnp.zeros_like(upper_part))

def factor_square(square):
    side = square.shape[0]
    positions = jnp.arange(side)

    def eliminate(column, packed):
        pivot_row = lax.dynamic_index_in_dim(packed, column, 0, keepdims=False)
        pivot_col = lax.dynamic_index_in_dim(packed, column, 1, keepdims=False)
        pivot_value = lax.dynamic_index_in_dim(pivot_row, column, 0, keepdims=False)
        under_mask = positions > column
        factor = jnp.where(under_mask, pivot_col / pivot_value, 0.0)
        right_row = jnp.where(under_mask, pivot_row, 0.0)
        packed = packed - factor[:, None] * right_row[None, :]
        return jnp.where((positions[None, :] == column) & under_mask[:, None], factor[:, None], packed)
    return lax.fori_loop(0, side, eliminate, square)

def factor_panel(square):
    panel_size = square.shape[0]
    block_width = min(16, panel_size)
    identity = jnp.eye(block_width, dtype=square.dtype)
    packed = square
    for first_col in range(0, panel_size, block_width):
        last_col = first_col + block_width
        diagonal = factor_square(packed[first_col:last_col, first_col:last_col])
        packed = packed.at[first_col:last_col, first_col:last_col].set(diagonal)
        if last_col < panel_size:
            lower_unit = jnp.tril(diagonal, -1) + identity
            upper_part = jnp.triu(diagonal)
            upper_inv = upper_inverse(upper_part)
            lower_inv = lower_unit_inverse(lower_unit)
            left_part = jnp.dot(packed[last_col:, first_col:last_col], upper_inv, precision=lax.Precision.HIGHEST)
            top_part = jnp.dot(lower_inv, packed[first_col:last_col, last_col:], precision=lax.Precision.HIGHEST)
            packed = packed.at[last_col:, first_col:last_col].set(left_part)
            packed = packed.at[first_col:last_col, last_col:].set(top_part)
            packed = packed.at[last_col:, last_col:].add(-jnp.dot(left_part, top_part, precision=lax.Precision.HIGHEST))
    return packed

def triangle_inverses(square):
    identity = jnp.eye(square.shape[0], dtype=square.dtype)
    packed = factor_panel(square)
    lower_unit = jnp.tril(packed, -1) + identity
    upper_part = jnp.triu(packed)
    return (upper_inverse(upper_part), lower_unit_inverse(lower_unit))

def reference(colloc_points, sources, counts, row_element, pivots):
    offset_x, offset_y = quad_offsets()

    def one_panel(column_tile):
        source = lax.dynamic_slice_in_dim(sources, column_tile * TILE_SIZE, TILE_SIZE, 1)
        tile_counts = lax.dynamic_index_in_dim(counts, column_tile, 1, keepdims=False)
        row_counts = jnp.repeat(tile_counts, TILE_SIZE, total_repeat_length=MATRIX_ORDER).astype(jnp.float32)
        running = jnp.zeros((MATRIX_ORDER, TILE_SIZE), jnp.float32)
        for quad_index in range(QUAD_MAX):
            weight = jnp.where(quad_index < row_counts, 1.0 / row_counts, 0.0)
            kernel_values = kelvin_entry(colloc_points[0][:, None], colloc_points[1][:, None], colloc_points[2][:, None], (source[0] + source[3] * offset_x[quad_index])[None, :], (source[1] + source[3] * offset_y[quad_index])[None, :], source[2][None, :], source[3][None, :])
            running = running + weight[:, None] * kernel_values
        return running
    panels = lax.map(one_panel, jnp.arange(COL_TILES))
    assembled = jnp.transpose(panels, (1, 0, 2)).reshape(MATRIX_ORDER, WINDOW_COLS)
    jump = jump_factor * TILE_SIZE
    column_ids = jnp.arange(WINDOW_COLS).astype(jnp.int32)
    matrix = assembled + jump * (row_element[:, None] == column_ids[None, :]).astype(jnp.float32)
    pivot_block = matrix[pivots]
    upper_inv, lower_inv = triangle_inverses(pivot_block[:, :TILE_SIZE])
    panel_factor = jnp.dot(matrix[:, :TILE_SIZE], upper_inv, precision=lax.Precision.HIGHEST, preferred_element_type=jnp.float32)
    u_rows = jnp.dot(lower_inv, pivot_block, precision=lax.Precision.HIGHEST, preferred_element_type=jnp.float32)
    factored = matrix - jnp.dot(panel_factor, u_rows, precision=lax.Precision.HIGHEST, preferred_element_type=jnp.float32)
    factored = factored.at[:, :TILE_SIZE].set(panel_factor)
    return (factored, u_rows)
```

```python
import jax
import jax.numpy as jnp
import numpy as np
from jax import lax
from jax.experimental import pallas as pl
from jax.experimental.pallas import tpu as pltpu
from jax.sharding import PartitionSpec as P

F32 = jnp.float32
BF = jnp.bfloat16
I32 = jnp.int32

TILE = 128
QUAD_MAX = 16
PAIRS = QUAD_MAX // 2
FEATS = 32
JUMP = 512.0
BLOCK = 16
GROUP = 6
JOBS = 8


def split3(v):
    high = v.astype(BF).astype(F32)
    rest = v - high
    mid = rest.astype(BF).astype(F32)
    low = (rest - mid).astype(BF).astype(F32)
    return high, mid, low


def mm(a, b):
    return jnp.dot(a, b, preferred_element_type=F32)


def mm32(a, b):
    return jnp.dot(a, b, precision=lax.Precision.HIGHEST, preferred_element_type=F32)


def point_features(x, y, z, extra):
    xs = x - 0.5
    ys = y - 0.5
    rows = []
    for v in (xs, ys, z):
        h, m, l = split3(v)
        rows += [h, h, m, m, h, l]
    rows += list(split3(xs * xs + ys * ys + z * z))
    one = jnp.ones_like(x)
    rows += [one, one, one]
    rows += extra
    zero = jnp.zeros_like(x)
    rows += [zero] * (FEATS - len(rows))
    rows = jnp.concatenate(rows, 0)
    return jnp.concatenate([rows, jnp.zeros((TILE - FEATS, TILE), F32)], 0)


def quad_offsets():
    numbers = np.arange(QUAD_MAX).astype(np.float32)
    radius = np.float32(4.0) * np.sqrt((numbers + np.float32(0.5)) / np.float32(QUAD_MAX))
    angles = np.float32(2.39996323) * numbers
    return radius * np.cos(angles), radius * np.sin(angles)


def build_table(s, wide_ref, tab_ref):
    off_x, off_y = quad_offsets()
    numbers = lax.broadcasted_iota(I32, (QUAD_MAX, TILE), 0)
    ox = jnp.zeros((QUAD_MAX, TILE), F32)
    oy = ox
    for q in range(QUAD_MAX):
        ox = jnp.where(numbers == q, float(off_x[q]), ox)
        oy = jnp.where(numbers == q, float(off_y[q]), oy)
    sx, sy, sz, size = [jnp.broadcast_to(s[i : i + 1], (QUAD_MAX, TILE)) for i in range(4)]
    ux = (sx + size * ox) - 0.5
    uy = (sy + size * oy) - 0.5
    norm = ux * ux + uy * uy + sz * sz + size * size
    wide_ref[...] = jnp.zeros_like(wide_ref)

    def put(f, v):
        wide_ref[pl.ds(f, QUAD_MAX, stride=FEATS), :] = v

    for base, u in ((0, -2.0 * ux), (6, -2.0 * uy), (12, -2.0 * sz)):
        uh, um, ul = split3(u)
        for k, v in enumerate((uh, um, uh, um, ul, uh)):
            put(base + k, v)
    one = jnp.ones((QUAD_MAX, TILE), F32)
    for k in range(3):
        put(18 + k, one)
    for k, v in enumerate(split3(norm)):
        put(21 + k, v)
    tab_ref[...] = jnp.zeros_like(tab_ref)
    rows = lax.broadcasted_iota(I32, (FEATS, TILE), 0)
    far = jnp.where(rows == 21, 1e30, 0.0).astype(BF)
    for q in range(QUAD_MAX):
        block = wide_ref[pl.ds(FEATS * q, FEATS), :].astype(BF)
        j = q // 2
        if q % 2 == 0:
            tab_ref[j, 0:FEATS, 0:TILE] = block
            tab_ref[PAIRS + j, 0:FEATS, 0:TILE] = block
            tab_ref[PAIRS + j, 0:FEATS, TILE:] = far
        else:
            tab_ref[j, 0:FEATS, TILE:] = block
    tab_ref[2 * PAIRS, 0:FEATS, 0:TILE] = far
    tab_ref[2 * PAIRS, 0:FEATS, TILE:] = far


def depth_rows(s):
    rows = lax.broadcasted_iota(I32, (FEATS, TILE), 0)
    zh, zm, zl = split3(jnp.broadcast_to(s[2:3], (FEATS, TILE)))
    dz = jnp.where((rows == 12) | (rows == 14) | (rows == 17), 1.0, 0.0)
    dz = jnp.where(rows == 21, -zh, dz)
    dz = jnp.where(rows == 22, -zm, dz)
    return jnp.where(rows == 23, -zl, dz)


def build_side(s, first_col, side_ref):
    rows = lax.broadcasted_iota(I32, (FEATS, TILE), 0)
    ids = (lax.broadcasted_iota(I32, (FEATS, TILE), 1) + first_col).astype(F32)
    high = jnp.floor(ids * (1.0 / 256.0))
    low = ids - 256.0 * high
    e = jnp.where(rows == 24, 256.0, 0.0)
    e = jnp.where(rows == 25, 1.0, e)
    e = jnp.where(rows == 21, -256.0 * high, e)
    e = jnp.where(rows == 22, -low, e)
    side_ref[...] = jnp.zeros_like(side_ref)
    side_ref[0:FEATS, 0:TILE] = depth_rows(s).astype(BF)
    side_ref[0:FEATS, TILE:] = e.astype(BF)


def tile_rows(t):
    return pl.ds(pl.multiple_of(t * TILE, TILE), TILE)


def kernel_sum(p, dz2):
    r = lax.rsqrt(p)
    value = r * (2.0 + dz2 * (r * r))
    return value


def prep_kernel(points, elements, lhs):
    tiles = points.shape[1] // TILE

    def group(g, carry):
        for k in range(GROUP):
            t = g * GROUP + k
            o = pl.multiple_of(t * TILE, TILE)
            pt = points[:, pl.ds(o, TILE)]
            re = elements[:, pl.ds(o, TILE)].astype(F32)
            high = jnp.floor(re * (1.0 / 256.0))
            f = point_features(pt[0:1], pt[1:2], pt[2:3], [high, re - 256.0 * high])
            lhs[pl.ds(o, TILE), :] = f.T.astype(BF)
        return carry

    lax.fori_loop(0, tiles // GROUP, group, 0)


def assemble_kernel(counts, lhs, sources, is_first, out, wide, tab, side, depth, *, first_tile):
    tiles = lhs.shape[0] // TILE
    s = sources[...]
    first_col = jnp.where(is_first, 0, lax.axis_index("col") * TILE)
    build_table(s, wide, tab)
    build_side(s, first_col, side)

    def start(g, carry):
        for k in range(GROUP):
            t = g * GROUP + k
            a = lhs[tile_rows(t), :]
            p = mm(a, tab[0])
            q = mm(a, side[...])
            n = jnp.full((1, TILE), counts[first_tile + t], I32).astype(F32)
            dz2 = q[:, 0:TILE] * q[:, 0:TILE]
            value = kernel_sum(p[:, 0:TILE], dz2) + kernel_sum(p[:, TILE:], dz2)
            out[tile_rows(t), :] = value + jnp.where(q[:, TILE:] == 0.0, JUMP * n, 0.0)
            depth[tile_rows(t), :] = dz2
        return carry

    lax.fori_loop(0, tiles // GROUP, start, 0)

    def count_jobs(t, total):
        return total + (counts[first_tile + t] - 1) // 2

    total = lax.fori_loop(0, tiles, count_jobs, 0)

    def skip(t):
        return t

    def jobs(i, state):
        t, j = state
        for _ in range(JOBS):
            tc = jnp.minimum(t, tiles - 1)
            n = counts[first_tile + tc]
            index = jnp.where(2 * j + 1 < n, j, PAIRS + j)
            index = jnp.where((t < tiles) & (2 * j < n), index, 2 * PAIRS)
            p = mm(lhs[tile_rows(tc), :], tab[index])
            dz2 = depth[tile_rows(tc), :]
            value = kernel_sum(p[:, 0:TILE], dz2) + kernel_sum(p[:, TILE:], dz2)
            out[tile_rows(tc), :] = out[tile_rows(tc), :] + value
            more = 2 * (j + 1) < n
            t = jnp.where(more, t, t + 1)
            j = jnp.where(more, j + 1, 1)
        return t, j

    def count_turns(t, total):
        return total + jnp.maximum((counts[first_tile + t] - 1) // 2, 1)

    turns = lax.fori_loop(0, tiles, count_turns, 0)
    lax.fori_loop(0, (turns + JOBS - 1) // JOBS, jobs, (0, 1))


def pick_kernel(points, pivots, own, root, out):
    tiles = points.shape[1] // TILE
    piv = jnp.broadcast_to(pivots[...], (8, TILE))
    tile = jnp.right_shift(piv, 7) - lax.axis_index("row") * tiles
    lane = jnp.bitwise_and(piv, TILE - 1)
    inside = (tile >= 0) & (tile < tiles)
    found = jnp.zeros((8, TILE), F32)
    for t in range(tiles):
        pt = jnp.concatenate([points[:, t * TILE : (t + 1) * TILE], jnp.zeros((5, TILE), F32)], 0)
        got = jnp.take_along_axis(pt, lane, axis=1, mode="promise_in_bounds")
        found = jnp.where(tile == t, got, found)
    at = jnp.clip(tile, 0, tiles - 1)
    own_counts = jnp.take_along_axis(own[...], at, axis=1, mode="promise_in_bounds")
    root_counts = jnp.take_along_axis(root[...], at, axis=1, mode="promise_in_bounds")
    rows = lax.broadcasted_iota(I32, (8, TILE), 0)
    own_counts = jnp.where(inside, jnp.broadcast_to(own_counts[4:5], (8, TILE)), 0.0)
    root_counts = jnp.where(inside, jnp.broadcast_to(root_counts[4:5], (8, TILE)), 0.0)
    found = jnp.where(rows == 3, own_counts, found)
    out[...] = jnp.where(rows == 4, root_counts, found)


def pivot_block(points, n_row, s, wide, tab, right):
    f = point_features(points[0:1], points[1:2], points[2:3], [n_row])
    a = f.T.astype(BF)
    build_table(s, wide, tab)
    rows = lax.broadcasted_iota(I32, (FEATS, TILE), 0)
    right[...] = jnp.zeros_like(right)
    right[0:FEATS, 0:TILE] = depth_rows(s).astype(BF)
    right[0:FEATS, TILE:] = jnp.where(rows == 24, 1.0, 0.0).astype(BF)
    q = mm(a, right[...])
    dz = q[:, 0:TILE]
    dz2 = dz * dz
    n = q[:, TILE:]
    total = jnp.zeros((TILE, TILE), F32)
    for j in range(PAIRS):
        p = mm(a, tab[j])
        for k in range(2):
            value = kernel_sum(p[:, k * TILE : (k + 1) * TILE], dz2)
            total = total + (value if 2 * j + k < 2 else jnp.where(n > 2 * j + k, value, 0.0))
    return total / n


def row_bcast(v, j, rows):
    return jnp.broadcast_to(v[j : j + 1, :], (rows, v.shape[1]))


def factor(x_ref, inv_ref, u_ref):
    side = TILE
    sub = lax.broadcasted_iota(I32, (BLOCK, TILE), 0)
    lane = lax.broadcasted_iota(I32, (BLOCK, TILE), 1)
    big = lax.broadcasted_iota(I32, (side, TILE), 0)
    inv_ref[...] = jnp.zeros_like(inv_ref)
    for b in range(side // BLOCK):
        k0 = b * BLOCK
        left = x_ref[k0 : k0 + BLOCK, 0:TILE]
        right = x_ref[k0 : k0 + BLOCK, TILE:]
        cols = [jnp.broadcast_to(left[:, k0 + j : k0 + j + 1], (BLOCK, TILE)) for j in range(BLOCK)]
        upper = jnp.zeros((BLOCK, TILE), F32)
        solved = jnp.zeros((BLOCK, TILE), F32)
        for j in range(BLOCK):
            f = cols[j]
            inv = 1.0 / row_bcast(f, j, BLOCK)
            vcol = jnp.where(sub == j, inv, jnp.where(sub < j, -f * inv, 0.0))
            upper = jnp.where(lane == k0 + j, vcol, upper)
            solved = jnp.where(sub == j, right, solved)
            here = sub == j

            def eliminate(v):
                row = row_bcast(v, j, BLOCK) * inv
                return jnp.where(here, row, v - f * row)

            for jj in range(j + 1, BLOCK):
                cols[jj] = eliminate(cols[jj])
            left = eliminate(left)
            right = eliminate(right)
        u_ref[k0 : k0 + BLOCK, :] = solved
        a = x_ref[:, 0:TILE]

        def rows_at(v):
            parts = []
            if k0:
                parts.append(jnp.zeros((k0, v.shape[1]), F32))
            parts.append(v)
            if k0 + BLOCK < side:
                parts.append(jnp.zeros((side - k0 - BLOCK, v.shape[1]), F32))
            return jnp.concatenate(parts, 0) if len(parts) > 1 else parts[0]

        t = rows_at(jnp.concatenate([left, right], 1))
        prod = mm32(a, t)
        mine = (big >= k0) & (big < k0 + BLOCK)
        x_ref[:, 0:TILE] = jnp.where(mine, t[:, 0:TILE], a - prod[:, 0:TILE])
        x_ref[:, TILE:] = jnp.where(mine, t[:, TILE:], x_ref[:, TILE:] - prod[:, TILE:])
        v = rows_at(upper)
        above = mm32(a, v)
        inv_ref[...] = inv_ref[...] + jnp.where(big < k0, -above, v)


def final_kernel(counts, counts_root, picked, sources, sources_root, own_hbm, root_hbm, out_hbm, u_out,
                 wide, tab, right, x, upper, w_ref, own, root, sems, out_sems):
    tiles = own.shape[0] // TILE
    own_copy = pltpu.make_async_copy(own_hbm, own, sems.at[0])
    root_copy = pltpu.make_async_copy(root_hbm, root, sems.at[1])
    own_copy.start()
    root_copy.start()
    is_root = lax.axis_index("col") == 0
    pk = picked[...]
    eye = (lax.broadcasted_iota(I32, (TILE, TILE), 0) == lax.broadcasted_iota(I32, (TILE, TILE), 1))
    x[:, 0:TILE] = pivot_block(pk, pk[4:5], sources_root[...], wide, tab, right) + jnp.where(eye, JUMP, 0.0)
    x[:, TILE:] = pivot_block(pk, pk[3:4], sources[...], wide, tab, right) + jnp.where(eye & is_root, JUMP, 0.0)
    factor(x, upper, u_out)
    w = jnp.where(is_root, upper[...], -x[:, TILE:])
    wh = w.astype(BF)
    wl = (w - wh.astype(F32)).astype(BF)
    w_ref[0:TILE, :] = wh
    w_ref[TILE : 2 * TILE, :] = wh
    w_ref[2 * TILE :, :] = wl
    own_copy.wait()
    root_copy.wait()
    copies = []

    def out_copy(g):
        rows = pl.ds(pl.multiple_of(g * (GROUP * TILE), TILE), GROUP * TILE)
        return pltpu.make_async_copy(own.at[rows, :], out_hbm.at[rows, :], out_sems.at[g])

    def group(g, carry):
        for k in range(GROUP):
            t = g * GROUP + k
            rows = tile_rows(t)
            n0 = jnp.full((1, TILE), counts_root[t], I32).astype(F32)
            nc = jnp.full((1, TILE), counts[t], I32).astype(F32)
            m0 = root[rows, :] * (1.0 / n0)
            h = m0.astype(BF)
            l = (m0 - h.astype(F32)).astype(BF)
            prod = mm(jnp.concatenate([h, l], 1), w_ref[0 : 2 * TILE, :]) + mm(h, w_ref[2 * TILE :, :])
            base = own[rows, :] * (1.0 / nc)
            own[rows, :] = jnp.where(is_root, prod, base + prod)
        out_copy(g).start()
        return carry

    lax.fori_loop(0, tiles // GROUP, group, 0)

    def finish(g, carry):
        out_copy(g).wait()
        return carry

    lax.fori_loop(0, tiles // GROUP, finish, 0)


def vmem():
    return pl.BlockSpec(memory_space=pltpu.VMEM)


def smem():
    return pl.BlockSpec(memory_space=pltpu.SMEM)


def hbm():
    return pl.BlockSpec(memory_space=pl.ANY)


def spread(value, axis, steps, sources_of):
    total = value
    for pairs in steps:
        total = total + lax.ppermute(value, axis, pairs)
    return total


def body(colloc_points, sources, counts, row_element, pivots):
    local_rows = colloc_points.shape[1]
    tiles = local_rows // TILE
    own_counts = counts.reshape(tiles)
    col = lax.axis_index("col")
    lhs = pl.pallas_call(
        prep_kernel,
        out_shape=jax.ShapeDtypeStruct((local_rows, TILE), BF),
        in_specs=[vmem(), vmem()],
        out_specs=vmem(),
        name="prep",
    )(colloc_points, row_element.reshape(1, local_rows))

    def assemble(which, tile_counts, tile_sources, name):
        import functools
        return pl.pallas_call(
            functools.partial(kernel_of_assembly, which=which),
            out_shape=jax.ShapeDtypeStruct((local_rows, TILE), F32),
            in_specs=[smem(), vmem(), vmem()],
            out_specs=vmem(),
            scratch_shapes=[
                pltpu.VMEM((QUAD_MAX * FEATS, TILE), F32),
                pltpu.VMEM((2 * PAIRS + 1, TILE, 2 * TILE), BF),
                pltpu.VMEM((TILE, 2 * TILE), BF),
                pltpu.VMEM((local_rows, TILE), F32),
            ],
            name=name,
        )(tile_counts, lhs, tile_sources)

    count_row = jnp.pad(own_counts.astype(F32)[None, :], ((0, 3), (0, TILE - tiles)))
    message = jnp.concatenate([sources, count_row], 0)
    y_part = jnp.where(col == 0, message, 0.0)
    for k in (2, 1, 3):
        y_part = y_part + lax.ppermute(message, "col", [(0, k)])
    x_part = jnp.where(col < 4, y_part, 0.0)
    for k in (8, 4, 12):
        x_part = x_part + lax.ppermute(y_part, "col", [(i, i + k) for i in range(4)])
    root_message = x_part
    own_sum = assemble(False, own_counts, sources, "own")
    root_sources = root_message[0:4]
    root_counts = root_message[4, :tiles].astype(I32)
    root_sum = assemble(True, root_counts, root_sources, "root")
    picked = pl.pallas_call(
        pick_kernel,
        out_shape=jax.ShapeDtypeStruct((8, TILE), F32),
        in_specs=[vmem()] * 4,
        out_specs=vmem(),
        name="pick",
    )(colloc_points, pivots.reshape(1, TILE), message, root_message)
    picked = picked + lax.ppermute(picked, "row", [(i, i ^ 1) for i in range(8)])
    base = picked
    for k in (4, 2, 6):
        picked = picked + lax.ppermute(base, "row", [(i, i ^ k) for i in range(8)])
    return pl.pallas_call(
        final_kernel,
        out_shape=(
            jax.ShapeDtypeStruct((local_rows, TILE), F32),
            jax.ShapeDtypeStruct((TILE, TILE), F32),
        ),
        in_specs=[smem(), smem(), vmem(), vmem(), vmem(), hbm(), hbm()],
        out_specs=(hbm(), vmem()),
        scratch_shapes=[
            pltpu.VMEM((QUAD_MAX * FEATS, TILE), F32),
            pltpu.VMEM((2 * PAIRS + 1, TILE, 2 * TILE), BF),
            pltpu.VMEM((TILE, 2 * TILE), BF),
            pltpu.VMEM((TILE, 2 * TILE), F32),
            pltpu.VMEM((TILE, TILE), F32),
            pltpu.VMEM((3 * TILE, TILE), BF),
            pltpu.VMEM((local_rows, TILE), F32),
            pltpu.VMEM((local_rows, TILE), F32),
            pltpu.SemaphoreType.DMA((2,)),
            pltpu.SemaphoreType.DMA((tiles // GROUP,)),
        ],
        name="final",
    )(own_counts, root_counts, picked, sources, root_sources, own_sum, root_sum)


def kernel_of_assembly(counts, lhs, sources, out, wide, tab, side, depth, *, which):
    assemble_kernel(counts, lhs, sources, which, out, wide, tab, side, depth, first_tile=0)


def solution(mesh):
    placed = (P(None, "row"), P(None, "col"), P("row", "col"), P("row"), P())
    return jax.shard_map(
        body,
        mesh=mesh,
        in_specs=placed,
        out_specs=(P("row", "col"), P(None, "col")),
        check_vma=False,
    )
```

```python
import functools

import jax
import jax.numpy as jnp
import numpy as np
from jax import lax
from jax.experimental import pallas as pl
from jax.experimental.pallas import tpu as pltpu
from jax.sharding import PartitionSpec as P


F32 = jnp.float32
BF = jnp.bfloat16
I32 = jnp.int32

TILE = 128
QUAD_MAX = 16
PAIRS = QUAD_MAX // 2
FEATS = 32
JUMP = 512.0
BLOCK = 16
GROUP = 10
JOBS = 8


def split3(v):
    high = v.astype(BF).astype(F32)
    rest = v - high
    mid = rest.astype(BF).astype(F32)
    low = (rest - mid).astype(BF).astype(F32)
    return high, mid, low


def mm(a, b):
    return jnp.dot(a, b, preferred_element_type=F32)


def halves(v):
    high = v.astype(BF)
    return high, (v - high.astype(F32)).astype(BF)


def mm3(a_high, a_low, b):
    b_high, b_low = halves(b)
    both = jnp.concatenate([a_high, a_low], 1)
    return mm(both, jnp.concatenate([b_high, b_high], 0)) + mm(a_high, b_low)


def point_features(x, y, z, extra):
    xs = x - 0.5
    ys = y - 0.5
    rows = []
    for v in (xs, ys, z):
        h, m, l = split3(v)
        rows += [h, h, m, m, h, l]
    rows += list(split3(xs * xs + ys * ys + z * z))
    one = jnp.ones_like(x)
    rows += [one, one, one]
    rows += extra
    zero = jnp.zeros_like(x)
    rows += [zero] * (FEATS - len(rows))
    rows = jnp.concatenate(rows, 0)
    return jnp.concatenate([rows, jnp.zeros((TILE - FEATS, TILE), F32)], 0)


def quad_offsets():
    numbers = np.arange(QUAD_MAX).astype(np.float32)
    radius = np.float32(4.0) * np.sqrt((numbers + np.float32(0.5)) / np.float32(QUAD_MAX))
    angles = np.float32(2.39996323) * numbers
    return radius * np.cos(angles), radius * np.sin(angles)


def build_table(s, wide_ref, tab_ref):
    off_x, off_y = quad_offsets()
    numbers = lax.broadcasted_iota(I32, (QUAD_MAX, TILE), 0)
    ox = jnp.zeros((QUAD_MAX, TILE), F32)
    oy = ox
    for q in range(QUAD_MAX):
        ox = jnp.where(numbers == q, float(off_x[q]), ox)
        oy = jnp.where(numbers == q, float(off_y[q]), oy)
    sx, sy, sz, size = [jnp.broadcast_to(s[i : i + 1], (QUAD_MAX, TILE)) for i in range(4)]
    ux = (sx + size * ox) - 0.5
    uy = (sy + size * oy) - 0.5
    norm = ux * ux + uy * uy + sz * sz + size * size
    wide_ref[...] = jnp.zeros_like(wide_ref)

    def put(f, v):
        wide_ref[pl.ds(f, QUAD_MAX, stride=FEATS), :] = v

    for base, u in ((0, -2.0 * ux), (6, -2.0 * uy), (12, -2.0 * sz)):
        uh, um, ul = split3(u)
        for k, v in enumerate((uh, um, uh, um, ul, uh)):
            put(base + k, v)
    one = jnp.ones((QUAD_MAX, TILE), F32)
    for k in range(3):
        put(18 + k, one)
    for k, v in enumerate(split3(norm)):
        put(21 + k, v)
    tab_ref[...] = jnp.zeros_like(tab_ref)
    rows = lax.broadcasted_iota(I32, (FEATS, TILE), 0)
    far = jnp.where(rows == 21, 1e30, 0.0).astype(BF)
    for q in range(QUAD_MAX):
        block = wide_ref[pl.ds(FEATS * q, FEATS), :].astype(BF)
        j = q // 2
        if q % 2 == 0:
            tab_ref[j, 0:FEATS, 0:TILE] = block
            tab_ref[PAIRS + j, 0:FEATS, 0:TILE] = block
            tab_ref[PAIRS + j, 0:FEATS, TILE:] = far
        else:
            tab_ref[j, 0:FEATS, TILE:] = block
    tab_ref[2 * PAIRS, 0:FEATS, 0:TILE] = far
    tab_ref[2 * PAIRS, 0:FEATS, TILE:] = far


def depth_rows(s):
    rows = lax.broadcasted_iota(I32, (FEATS, TILE), 0)
    zh, zm, zl = split3(jnp.broadcast_to(s[2:3], (FEATS, TILE)))
    dz = jnp.where((rows == 12) | (rows == 14) | (rows == 17), 1.0, 0.0)
    dz = jnp.where(rows == 21, -zh, dz)
    dz = jnp.where(rows == 22, -zm, dz)
    return jnp.where(rows == 23, -zl, dz)


def build_side(s, first_col, side_ref):
    rows = lax.broadcasted_iota(I32, (FEATS, TILE), 0)
    ids = (lax.broadcasted_iota(I32, (FEATS, TILE), 1) + first_col).astype(F32)
    high = jnp.floor(ids * (1.0 / 256.0))
    low = ids - 256.0 * high
    e = jnp.where(rows == 24, 256.0, 0.0)
    e = jnp.where(rows == 25, 1.0, e)
    e = jnp.where(rows == 21, -256.0 * high, e)
    e = jnp.where(rows == 22, -low, e)
    side_ref[...] = jnp.zeros_like(side_ref)
    side_ref[0:FEATS, 0:TILE] = depth_rows(s).astype(BF)
    side_ref[0:FEATS, TILE:] = e.astype(BF)


def tile_rows(t):
    return pl.ds(pl.multiple_of(t * TILE, TILE), TILE)


def kernel_sum(p, dz2):
    r = lax.rsqrt(p)
    value = r * (2.0 + dz2 * (r * r))
    return value


def pair_sum(p, half):
    r = lax.rsqrt(p)
    cube = r * (r * r)
    return (r[:, 0:TILE] + r[:, TILE:]) + half * (cube[:, 0:TILE] + cube[:, TILE:])


def prep_kernel(points, elements, lhs):
    tiles = points.shape[1] // TILE

    def group(g, carry):
        for k in range(GROUP):
            t = g * GROUP + k
            o = pl.multiple_of(t * TILE, TILE)
            pt = points[:, pl.ds(o, TILE)]
            re = elements[pl.ds(t, 1), :].astype(F32)
            high = jnp.floor(re * (1.0 / 256.0))
            f = point_features(pt[0:1], pt[1:2], pt[2:3], [high, re - 256.0 * high])
            lhs[pl.ds(o, TILE), :] = f.T.astype(BF)
        return carry

    lax.fori_loop(0, tiles // GROUP, group, 0)


def assemble(count, lhs, out, tab, side, depth, ahead, first_tile):
    tiles = out.shape[0] // TILE

    def start(g, carry):
        for k in range(GROUP):
            t = g * GROUP + k
            a = lhs[tile_rows(first_tile + t), :]
            p = mm(a, tab[0])
            q = mm(a, side[...])
            n = jnp.full((1, TILE), count(first_tile + t), I32).astype(F32)
            half = q[:, 0:TILE] * (q[:, 0:TILE] * 0.5)
            out[tile_rows(t), :] = pair_sum(p, half) + jnp.where(q[:, TILE:] == 0.0, (0.5 * JUMP) * n, 0.0)
            depth[tile_rows(t), :] = half
        return carry

    lax.fori_loop(0, tiles // GROUP, start, 0)

    def fill(slot, t, j):
        tc = jnp.minimum(t, tiles - 1)
        n = count(first_tile + tc)
        index = jnp.where(2 * j + 1 < n, j, PAIRS + j)
        index = jnp.where((t < tiles) & (2 * j < n), index, 2 * PAIRS)
        ahead[slot] = mm(lhs[tile_rows(first_tile + tc), :], tab[index])
        more = 2 * (j + 1) < n
        short = count(first_tile + jnp.minimum(t + 1, tiles - 1)) <= 2
        return tc, jnp.where(more, t, jnp.where(short, t + 2, t + 1)), jnp.where(more, j + 1, 1)

    def fill_all(t, j):
        at = []
        for slot in range(JOBS):
            tc, t, j = fill(slot, t, j)
            at.append(tc)
        return t, j, tuple(at)

    def jobs(state):
        _, t, j, at = state
        for slot in range(JOBS):
            rows = tile_rows(at[slot])
            out[rows, :] = out[rows, :] + pair_sum(ahead[slot], depth[rows, :])
        return (t,) + fill_all(t, j)

    first = jnp.where(count(first_tile) <= 2, 1, 0)
    lax.while_loop(lambda state: state[0] < tiles, jobs, (first,) + fill_all(first, 1))


def own_kernel(counts, lhs, sources, out, tab, side, wide, depth, ahead):
    s = sources[...]
    build_table(s, wide, tab)
    build_side(s, lax.axis_index("col") * TILE, side)
    assemble(lambda t: counts[t], lhs, out, tab, side, depth, ahead, 0)


def rest_kernel(counts, lhs, tab, side, out, depth, ahead, *, first_tile):
    assemble(lambda t: counts[t], lhs, out, tab, side, depth, ahead, first_tile)


def root_kernel(message_scalars, lhs, message, out, tab, side, wide, depth, ahead):
    s = message[0:4]
    build_table(s, wide, tab)
    build_side(s, 0, side)
    assemble(lambda t: message_scalars[4, t].astype(I32), lhs, out, tab, side, depth, ahead, 0)


def pick_kernel(points, pivots, own, root, out):
    tiles = points.shape[1] // TILE
    piv = jnp.broadcast_to(pivots[...], (8, TILE))
    tile = jnp.right_shift(piv, 7) - lax.axis_index("row") * tiles
    lane = jnp.bitwise_and(piv, TILE - 1)
    inside = (tile >= 0) & (tile < tiles)
    found = jnp.zeros((8, TILE), F32)
    for t in range(tiles):
        pt = jnp.concatenate([points[:, t * TILE : (t + 1) * TILE], jnp.zeros((5, TILE), F32)], 0)
        got = jnp.take_along_axis(pt, lane, axis=1, mode="promise_in_bounds")
        found = jnp.where(tile == t, got, found)
    at = jnp.clip(tile, 0, tiles - 1)
    own_counts = jnp.take_along_axis(own[...], at, axis=1, mode="promise_in_bounds")
    root_counts = jnp.take_along_axis(root[...], at, axis=1, mode="promise_in_bounds")
    rows = lax.broadcasted_iota(I32, (8, TILE), 0)
    own_counts = jnp.where(inside, jnp.broadcast_to(own_counts[4:5], (8, TILE)), 0.0)
    root_counts = jnp.where(inside, jnp.broadcast_to(root_counts[4:5], (8, TILE)), 0.0)
    found = jnp.where(rows == 3, own_counts, found)
    out[...] = jnp.where(rows == 4, root_counts, found)


def pivot_block(points, n_row, tab, side, right):
    f = point_features(points[0:1], points[1:2], points[2:3], [n_row])
    a = f.T.astype(BF)
    right[:, 0:TILE] = side[:, 0:TILE]
    q = mm(a, right[...])
    dz = q[:, 0:TILE]
    dz2 = dz * dz
    n = q[:, TILE:]
    total = jnp.zeros((TILE, TILE), F32)
    for j in range(PAIRS):
        p = mm(a, tab[j])
        for k in range(2):
            value = kernel_sum(p[:, k * TILE : (k + 1) * TILE], dz2)
            total = total + (value if 2 * j + k < 2 else jnp.where(n > 2 * j + k, value, 0.0))
    return total / n


def row_bcast(v, j, rows):
    return jnp.broadcast_to(v[j : j + 1, :], (rows, v.shape[1]))


def factor(x_ref, inv_ref, u_ref):
    side = TILE
    sub = lax.broadcasted_iota(I32, (BLOCK, TILE), 0)
    lane = lax.broadcasted_iota(I32, (BLOCK, TILE), 1)
    big = lax.broadcasted_iota(I32, (side, TILE), 0)
    inv_ref[...] = jnp.zeros_like(inv_ref)
    for b in range(side // BLOCK):
        k0 = b * BLOCK
        left = x_ref[k0 : k0 + BLOCK, 0:TILE]
        right = x_ref[k0 : k0 + BLOCK, TILE:]
        cols = [jnp.broadcast_to(left[:, k0 + j : k0 + j + 1], (BLOCK, TILE)) for j in range(BLOCK)]
        upper = jnp.zeros((BLOCK, TILE), F32)
        solved = jnp.zeros((BLOCK, TILE), F32)
        for j in range(BLOCK):
            f = cols[j]
            inv = 1.0 / row_bcast(f, j, BLOCK)
            vcol = jnp.where(sub == j, inv, jnp.where(sub < j, -f * inv, 0.0))
            upper = jnp.where(lane == k0 + j, vcol, upper)
            solved = jnp.where(sub == j, right, solved)
            here = sub == j

            def eliminate(v):
                row = row_bcast(v, j, BLOCK) * inv
                return jnp.where(here, row, v - f * row)

            for jj in range(j + 1, BLOCK):
                cols[jj] = eliminate(cols[jj])
            left = eliminate(left)
            right = eliminate(right)
        u_ref[k0 : k0 + BLOCK, :] = solved
        a = x_ref[:, 0:TILE]

        def rows_at(v):
            parts = []
            if k0:
                parts.append(jnp.zeros((k0, v.shape[1]), F32))
            parts.append(v)
            if k0 + BLOCK < side:
                parts.append(jnp.zeros((side - k0 - BLOCK, v.shape[1]), F32))
            return jnp.concatenate(parts, 0) if len(parts) > 1 else parts[0]

        t = rows_at(jnp.concatenate([left, right], 1))
        a_high, a_low = halves(a)
        prod = mm3(a_high, a_low, t)
        mine = (big >= k0) & (big < k0 + BLOCK)
        x_ref[:, 0:TILE] = jnp.where(mine, t[:, 0:TILE], a - prod[:, 0:TILE])
        x_ref[:, TILE:] = jnp.where(mine, t[:, TILE:], x_ref[:, TILE:] - prod[:, TILE:])
        v = rows_at(upper)
        above = mm3(a_high, a_low, v)
        inv_ref[...] = inv_ref[...] + jnp.where(big < k0, -above, v)


def final_kernel(counts, message, picked, own_tab, own_side, root_tab, root_side, own, rest, root,
                 out_hbm, u_out, right, x, upper, w_ref, ready, out_sems):
    tiles = root.shape[0] // TILE
    early = own.shape[0] // TILE
    is_root = lax.axis_index("col") == 0
    pk = picked[...]
    eye = (lax.broadcasted_iota(I32, (TILE, TILE), 0) == lax.broadcasted_iota(I32, (TILE, TILE), 1))
    right[:, TILE:] = jnp.where(lax.broadcasted_iota(I32, (TILE, TILE), 0) == 24, 1.0, 0.0).astype(BF)
    x[:, 0:TILE] = pivot_block(pk, pk[4:5], root_tab, root_side, right) + jnp.where(eye, JUMP, 0.0)
    x[:, TILE:] = pivot_block(pk, pk[3:4], own_tab, own_side, right) + jnp.where(eye & is_root, JUMP, 0.0)
    factor(x, upper, u_out)
    w = jnp.where(is_root, upper[...], -x[:, TILE:])
    wh = w.astype(BF)
    wl = (w - wh.astype(F32)).astype(BF)
    w_ref[0:TILE, :] = wh
    w_ref[TILE : 2 * TILE, :] = wh
    w_ref[2 * TILE :, :] = wl
    keep = jnp.where(is_root, 0.0, 2.0)

    def out_copy(g):
        rows = pl.ds(pl.multiple_of(g * (GROUP * TILE), TILE), GROUP * TILE)
        return pltpu.make_async_copy(ready.at[rows, :], out_hbm.at[rows, :], out_sems.at[g])

    def part(block, first):
        def group(g, carry):
            for k in range(GROUP):
                at = g * GROUP + k
                t = first + at
                rows = tile_rows(t)
                n0 = jnp.full((1, TILE), message[4, t], F32)
                nc = jnp.full((1, TILE), counts[t], I32).astype(F32)
                h, l = halves(root[rows, :] * (2.0 / n0))
                prod = mm(jnp.concatenate([h, l], 1), w_ref[0 : 2 * TILE, :]) + mm(h, w_ref[2 * TILE :, :])
                ready[rows, :] = block[tile_rows(at), :] * (keep / nc) + prod
            out_copy(first // GROUP + g).start()
            return carry

        lax.fori_loop(0, block.shape[0] // TILE // GROUP, group, 0)

    part(own, 0)
    part(rest, early)

    def finish(g, carry):
        out_copy(g).wait()
        return carry

    lax.fori_loop(0, tiles // GROUP, finish, 0)


def vmem():
    return pl.BlockSpec(memory_space=pltpu.VMEM)


def smem():
    return pl.BlockSpec(memory_space=pltpu.SMEM)


def hbm():
    return pl.BlockSpec(memory_space=pl.ANY)


def numbered(send, steps):
    parts = []
    for k in steps:
        parts.append(send(k))
    return parts


def limit(mib):
    return pltpu.CompilerParams(vmem_limit_bytes=mib * 1024 * 1024)


def steps(colloc_points, sources, counts, row_element, pivots):
    local_rows = colloc_points.shape[1]
    tiles = local_rows // TILE
    early = tiles // 2
    own_counts = counts.reshape(tiles)
    col = lax.axis_index("col")
    table = jax.ShapeDtypeStruct((2 * PAIRS + 1, TILE, 2 * TILE), BF)
    aside = jax.ShapeDtypeStruct((TILE, 2 * TILE), BF)

    def part(count):
        return jax.ShapeDtypeStruct((count * TILE, TILE), F32)

    wide = pltpu.VMEM((QUAD_MAX * FEATS, TILE), F32)

    def work(count):
        return [pltpu.VMEM((count * TILE, TILE), F32), pltpu.VMEM((JOBS, TILE, 2 * TILE), F32)]

    count_row = jnp.pad(own_counts.astype(F32)[None, :], ((0, 3), (0, TILE - tiles)))
    message = jnp.concatenate([sources, count_row], 0)
    got = numbered(lambda k: lax.ppermute(message, "col", [(0, k)]), (2, 1, 3))
    y_part = jnp.where(col == 0, message, got[0] + got[1] + got[2])
    got = numbered(lambda k: lax.ppermute(y_part, "col", [(i, i + k) for i in range(4)]), (8, 4, 12))
    root_message = jnp.where(col < 4, y_part, got[0] + got[1] + got[2])
    lhs = pl.pallas_call(
        prep_kernel,
        out_shape=jax.ShapeDtypeStruct((local_rows, TILE), BF),
        in_specs=[vmem(), vmem()],
        out_specs=vmem(),
        compiler_params=limit(8),
        name="prep",
    )(colloc_points, row_element.reshape(tiles, TILE))
    own_sum, own_tab, own_side = pl.pallas_call(
        own_kernel,
        out_shape=(part(early), table, aside),
        in_specs=[smem(), vmem(), vmem()],
        out_specs=(vmem(), vmem(), vmem()),
        scratch_shapes=[wide] + work(early),
        compiler_params=limit(12),
        name="own",
    )(own_counts, lhs, sources)
    picked = pl.pallas_call(
        pick_kernel,
        out_shape=jax.ShapeDtypeStruct((8, TILE), F32),
        in_specs=[vmem()] * 4,
        out_specs=vmem(),
        compiler_params=limit(4),
        name="pick",
    )(colloc_points, pivots.reshape(1, TILE), message, root_message)
    picked = picked + lax.ppermute(picked, "row", [(i, i ^ 1) for i in range(8)])
    got = numbered(lambda k: lax.ppermute(picked, "row", [(i, i ^ k) for i in range(8)]), (4, 2, 6))
    picked = picked + got[0] + got[1] + got[2]
    rest_sum = pl.pallas_call(
        functools.partial(rest_kernel, first_tile=early),
        out_shape=part(tiles - early),
        in_specs=[smem(), vmem(), vmem(), vmem()],
        out_specs=vmem(),
        scratch_shapes=work(tiles - early),
        compiler_params=limit(12),
        name="rest",
    )(own_counts, lhs, own_tab, own_side)
    root_sum, root_tab, root_side = pl.pallas_call(
        root_kernel,
        out_shape=(part(tiles), table, aside),
        in_specs=[smem(), vmem(), vmem()],
        out_specs=(vmem(), vmem(), vmem()),
        scratch_shapes=[wide] + work(tiles),
        compiler_params=limit(18),
        name="root",
    )(root_message, lhs, root_message)
    return pl.pallas_call(
        final_kernel,
        out_shape=(
            jax.ShapeDtypeStruct((local_rows, TILE), F32),
            jax.ShapeDtypeStruct((TILE, TILE), F32),
        ),
        in_specs=[smem(), smem()] + [vmem()] * 8,
        out_specs=(hbm(), vmem()),
        scratch_shapes=[
            pltpu.VMEM((TILE, 2 * TILE), BF),
            pltpu.VMEM((TILE, 2 * TILE), F32),
            pltpu.VMEM((TILE, TILE), F32),
            pltpu.VMEM((3 * TILE, TILE), BF),
            pltpu.VMEM((local_rows, TILE), F32),
            pltpu.SemaphoreType.DMA((tiles // GROUP,)),
        ],
        compiler_params=limit(16),
        name="final",
    )(own_counts, root_message, picked, own_tab, own_side, root_tab, root_side, own_sum, rest_sum, root_sum)


def solution(mesh):
    placed = (P(None, "row"), P(None, "col"), P("row", "col"), P("row"), P())
    return jax.shard_map(
        steps,
        mesh=mesh,
        in_specs=placed,
        out_specs=(P("row", "col"), P(None, "col")),
        check_vma=False,
    )
```

```python
import functools

import jax
import jax.numpy as jnp
import numpy as np
from jax import lax
from jax.experimental import pallas as pl
from jax.experimental.pallas import tpu as pltpu
from jax.sharding import PartitionSpec as P


F32 = jnp.float32
BF = jnp.bfloat16
I32 = jnp.int32

TILE = 128
QUAD_MAX = 16
PAIRS = QUAD_MAX // 2
FEATS = 32
JUMP = 512.0
BLOCK = 16
GROUP = 10
JOBS = 8
DEPTH = 256
WAYS = 6


def split3(v):
    high = v.astype(BF).astype(F32)
    rest = v - high
    mid = rest.astype(BF).astype(F32)
    low = (rest - mid).astype(BF).astype(F32)
    return high, mid, low


def mm(a, b):
    return jnp.dot(a, b, preferred_element_type=F32)


def halves(v):
    high = v.astype(BF)
    return high, (v - high.astype(F32)).astype(BF)


def point_features(x, y, z, extra):
    xs = x - 0.5
    ys = y - 0.5
    rows = []
    for v in (xs, ys, z):
        h, m, l = split3(v)
        rows += [h, h, m, m, h, l]
    rows += list(split3(xs * xs + ys * ys + z * z))
    one = jnp.ones_like(x)
    rows += [one, one, one]
    rows += extra
    zero = jnp.zeros_like(x)
    rows += [zero] * (FEATS - len(rows))
    rows = jnp.concatenate(rows, 0)
    return jnp.concatenate([rows, jnp.zeros((TILE - FEATS, TILE), F32)], 0)


def quad_offsets():
    numbers = np.arange(QUAD_MAX).astype(np.float32)
    radius = np.float32(4.0) * np.sqrt((numbers + np.float32(0.5)) / np.float32(QUAD_MAX))
    angles = np.float32(2.39996323) * numbers
    return radius * np.cos(angles), radius * np.sin(angles)


def build_table(s, wide_ref, tab_ref):
    off_x, off_y = quad_offsets()
    numbers = lax.broadcasted_iota(I32, (QUAD_MAX, TILE), 0)
    ox = jnp.zeros((QUAD_MAX, TILE), F32)
    oy = ox
    for q in range(QUAD_MAX):
        ox = jnp.where(numbers == q, float(off_x[q]), ox)
        oy = jnp.where(numbers == q, float(off_y[q]), oy)
    sx, sy, sz, size = [jnp.broadcast_to(s[i : i + 1], (QUAD_MAX, TILE)) for i in range(4)]
    ux = (sx + size * ox) - 0.5
    uy = (sy + size * oy) - 0.5
    norm = ux * ux + uy * uy + sz * sz + size * size
    wide_ref[...] = jnp.zeros_like(wide_ref)

    def put(f, v):
        wide_ref[pl.ds(f, QUAD_MAX, stride=FEATS), :] = v

    for base, u in ((0, -2.0 * ux), (6, -2.0 * uy), (12, -2.0 * sz)):
        uh, um, ul = split3(u)
        for k, v in enumerate((uh, um, uh, um, ul, uh)):
            put(base + k, v)
    one = jnp.ones((QUAD_MAX, TILE), F32)
    for k in range(3):
        put(18 + k, one)
    for k, v in enumerate(split3(norm)):
        put(21 + k, v)
    rows = lax.broadcasted_iota(I32, (FEATS, TILE), 0)
    far = jnp.where(rows == 21, 1e30, 0.0).astype(BF)
    for q in range(QUAD_MAX):
        block = wide_ref[pl.ds(FEATS * q, FEATS), :].astype(BF)
        j = q // 2
        if q % 2 == 0:
            tab_ref[j, 0:FEATS, 0:TILE] = block
            tab_ref[PAIRS + j, 0:FEATS, 0:TILE] = block
            tab_ref[PAIRS + j, 0:FEATS, TILE:] = far
        else:
            tab_ref[j, 0:FEATS, TILE:] = block
    tab_ref[2 * PAIRS, 0:FEATS, 0:TILE] = far
    tab_ref[2 * PAIRS, 0:FEATS, TILE:] = far


def depth_rows(s):
    rows = lax.broadcasted_iota(I32, (FEATS, TILE), 0)
    zh, zm, zl = split3(jnp.broadcast_to(s[2:3], (FEATS, TILE)))
    dz = jnp.where((rows == 12) | (rows == 14) | (rows == 17), 1.0, 0.0)
    dz = jnp.where(rows == 21, -zh, dz)
    dz = jnp.where(rows == 22, -zm, dz)
    return jnp.where(rows == 23, -zl, dz)


def build_side(s, first_col, side_ref):
    rows = lax.broadcasted_iota(I32, (FEATS, TILE), 0)
    ids = (lax.broadcasted_iota(I32, (FEATS, TILE), 1) + first_col).astype(F32)
    high = jnp.floor(ids * (1.0 / 256.0))
    low = ids - 256.0 * high
    e = jnp.where(rows == 24, 256.0, 0.0)
    e = jnp.where(rows == 25, 1.0, e)
    e = jnp.where(rows == 21, -256.0 * high, e)
    e = jnp.where(rows == 22, -low, e)
    side_ref[0:FEATS, 0:TILE] = depth_rows(s).astype(BF)
    side_ref[0:FEATS, TILE:] = e.astype(BF)


def tile_rows(t):
    return pl.ds(pl.multiple_of(t * TILE, TILE), TILE)


def kernel_sum(p, dz2):
    r = lax.rsqrt(p)
    value = r * (2.0 + dz2 * (r * r))
    return value


def pair_sum(p, half):
    r = lax.rsqrt(p)
    cube = r * (r * r)
    return (r[:, 0:TILE] + r[:, TILE:]) + half * (cube[:, 0:TILE] + cube[:, TILE:])


def build_lhs(points, elements, lhs):
    tiles = points.shape[1] // TILE

    def group(g, carry):
        for k in range(GROUP):
            t = g * GROUP + k
            o = pl.multiple_of(t * TILE, TILE)
            pt = points[:, pl.ds(o, TILE)]
            re = elements[pl.ds(t, 1), :].astype(F32)
            high = jnp.floor(re * (1.0 / 256.0))
            f = point_features(pt[0:1], pt[1:2], pt[2:3], [high, re - 256.0 * high])
            lhs[pl.ds(o, TILE), :] = f.T.astype(BF)
        return carry

    lax.fori_loop(0, tiles // GROUP, group, 0)


def pack_kernel(sources_hbm, counts_hbm, out, counts, sems):
    loads = [
        pltpu.make_async_copy(sources_hbm, out.at[pl.ds(0, 4), :], sems.at[0]),
        pltpu.make_async_copy(counts_hbm, counts, sems.at[1]),
    ]
    for load in loads:
        load.start()
    out[4:, :] = jnp.zeros((4, TILE), F32)
    for load in loads:
        load.wait()
    out[4:5, 0 : counts.shape[1]] = counts[...].astype(F32)


def wide_lhs(a):
    return jnp.concatenate([a, jnp.zeros((a.shape[0], DEPTH - a.shape[1]), BF)], 1)


def tall(b, rows):
    return jnp.concatenate([b, jnp.zeros((rows - b.shape[0], b.shape[1]), BF)], 0)


def send(acc, a, b, slot):
    pltpu.matmul_push_rhs(tall(b, DEPTH), slot // 2 % 2, slot % 2)
    pltpu.matmul_acc_lhs(acc, wide_lhs(a), load_staged_rhs=slot // 2 % 2)


def assemble(count, lhs, out, tab, side, depth, first_tile, *accs):
    tiles = out.shape[0] // TILE

    def begin(slot, t):
        a = lhs[tile_rows(first_tile + jnp.minimum(t, tiles - 1)), :]
        send(accs[2 * slot], a, tab[0], 2 * slot)
        send(accs[2 * slot + 1], a, side[...], 2 * slot + 1)

    def finish(slot, t):
        p = pltpu.matmul_pop(accs[2 * slot])
        q = pltpu.matmul_pop(accs[2 * slot + 1])
        n = jnp.full((1, TILE), count(first_tile + t), I32).astype(F32)
        half = q[:, 0:TILE] * (q[:, 0:TILE] * 0.5)
        out[tile_rows(t), :] = pair_sum(p, half) + jnp.where(q[:, TILE:] == 0.0, (0.5 * JUMP) * n, 0.0)
        depth[tile_rows(t), :] = half

    ways = JOBS // 2
    for slot in range(ways):
        begin(slot, slot)

    def start(g, carry):
        for slot in range(ways):
            t = g * ways + slot
            finish(slot, jnp.minimum(t, tiles - 1))
            begin(slot, t + ways)
        return carry

    lax.fori_loop(0, (tiles + ways - 1) // ways, start, 0)
    for acc in accs:
        pltpu.matmul_pop(acc)

    def fill(slot, t, j):
        tc = jnp.minimum(t, tiles - 1)
        n = count(first_tile + tc)
        index = jnp.where(2 * j + 1 < n, j, PAIRS + j)
        index = jnp.where((t < tiles) & (2 * j < n), index, 2 * PAIRS)
        send(accs[slot], lhs[tile_rows(first_tile + tc), :], tab[index], slot)
        more = 2 * (j + 1) < n
        short = count(first_tile + jnp.minimum(t + 1, tiles - 1)) <= 2
        return tc, jnp.where(more, t, jnp.where(short, t + 2, t + 1)), jnp.where(more, j + 1, 1)

    def jobs(state):
        _, t, j, at = state
        upcoming = []
        at_start = t
        for slot in range(JOBS):
            rows = tile_rows(at[slot])
            p = pltpu.matmul_pop(accs[slot])
            out[rows, :] = out[rows, :] + pair_sum(p, depth[rows, :])
            tc, t, j = fill(slot, t, j)
            upcoming.append(tc)
        return at_start, t, j, tuple(upcoming)

    first = jnp.where(count(first_tile) <= 2, 1, 0)
    t, j = first, 1
    at = []
    for slot in range(JOBS):
        tc, t, j = fill(slot, t, j)
        at.append(tc)
    lax.while_loop(lambda state: state[0] < tiles, jobs, (first, t, j, tuple(at)))
    for acc in accs:
        pltpu.matmul_pop(acc)


def own_kernel(counts_hbm, points_hbm, elements_hbm, pivots_hbm, message, out, lhs, tab, side, found,
               counts, points, elements, pivots, wide, depth, sems, *, accs):
    loads = [
        pltpu.make_async_copy(points_hbm, points, sems.at[0]),
        pltpu.make_async_copy(elements_hbm, elements, sems.at[1]),
        pltpu.make_async_copy(pivots_hbm, pivots, sems.at[2]),
        pltpu.make_async_copy(counts_hbm, counts, sems.at[3]),
    ]
    for load in loads:
        load.start()
    s = message[0:4]
    build_table(s, wide, tab)
    build_side(s, lax.axis_index("col") * TILE, side)
    for load in loads:
        load.wait()
    build_lhs(points, elements, lhs)
    find_pivots(points, pivots, message, found)
    pl.run_scoped(functools.partial(assemble, lambda t: counts[t], lhs, out, tab, side, depth, 0), *accs)


def rest_kernel(counts_hbm, lhs, message, own_tab, own_side, rest_out, root_out, tab, side,
                counts, scalars, wide, depth, sems, *, accs):
    loads = [
        pltpu.make_async_copy(counts_hbm, counts, sems.at[0]),
        pltpu.make_async_copy(message, scalars, sems.at[1]),
    ]
    for load in loads:
        load.start()
    s = message[0:4]
    build_table(s, wide, tab)
    build_side(s, 0, side)
    for load in loads:
        load.wait()
    early = (lhs.shape[0] - rest_out.shape[0]) // TILE

    def both(*accs):
        assemble(lambda t: counts[t], lhs, rest_out, own_tab, own_side, depth, early, *accs)
        assemble(lambda t: scalars[4, t].astype(I32), lhs, root_out, tab, side, depth, 0, *accs)

    pl.run_scoped(both, *accs)


def find_pivots(points, pivots, message, out):
    tiles = points.shape[1] // TILE
    piv = jnp.broadcast_to(pivots[...], (8, TILE))
    tile = jnp.right_shift(piv, 7) - lax.axis_index("row") * tiles
    lane = jnp.bitwise_and(piv, TILE - 1)
    inside = (tile >= 0) & (tile < tiles)
    found = jnp.zeros((8, TILE), F32)
    for t in range(tiles):
        pt = jnp.concatenate([points[:, t * TILE : (t + 1) * TILE], jnp.zeros((5, TILE), F32)], 0)
        got = jnp.take_along_axis(pt, lane, axis=1, mode="promise_in_bounds")
        found = jnp.where(tile == t, got, found)
    at = jnp.clip(tile, 0, tiles - 1)
    count = jnp.take_along_axis(message[...], at, axis=1, mode="promise_in_bounds")
    rows = lax.broadcasted_iota(I32, (8, TILE), 0)
    found = jnp.where((rows == 3) & inside, jnp.broadcast_to(count[4:5], (8, TILE)), found)
    out[...] = jnp.where((rows == 4) & inside, (tile + 1).astype(F32), found)


def pick_kernel(found, root, out):
    tile = jnp.broadcast_to(found[4:5], (8, TILE))
    at = jnp.maximum(tile.astype(I32) - 1, 0)
    count = jnp.take_along_axis(root[...], at, axis=1, mode="promise_in_bounds")
    rows = lax.broadcasted_iota(I32, (8, TILE), 0)
    count = jnp.where(tile > 0.0, jnp.broadcast_to(count[4:5], (8, TILE)), 0.0)
    out[...] = jnp.where(rows == 4, count, found[...])


def pivot_block(points, n_row, tab, side, right):
    f = point_features(points[0:1], points[1:2], points[2:3], [n_row])
    a = f.T.astype(BF)
    right[0:FEATS, 0:TILE] = side[:, 0:TILE]
    q = mm(a, right[...])
    dz = q[:, 0:TILE]
    dz2 = dz * dz
    n = q[:, TILE:]
    total = jnp.zeros((TILE, TILE), F32)
    for j in range(PAIRS):
        p = mm(a, tall(tab[j], TILE))
        for k in range(2):
            value = kernel_sum(p[:, k * TILE : (k + 1) * TILE], dz2)
            total = total + (value if 2 * j + k < 2 else jnp.where(n > 2 * j + k, value, 0.0))
    return total / n


def factor(x_ref, inv_ref, u_ref):
    side = TILE
    half = 8
    sub = lax.broadcasted_iota(I32, (half, TILE), 0)
    lane = lax.broadcasted_iota(I32, (half, TILE), 1)
    big = lax.broadcasted_iota(I32, (side, TILE), 0)
    inv_ref[...] = jnp.zeros_like(inv_ref)
    parts = range(BLOCK // half)

    def whole(rows):
        return jnp.broadcast_to(rows, (half, TILE))

    for b in range(side // BLOCK):
        k0 = b * BLOCK
        block = x_ref[:, k0 : k0 + BLOCK]
        high = block.astype(BF).astype(F32)
        a = jnp.concatenate([high, block - high, high], 1).astype(BF)
        left = [x_ref[k0 + half * i : k0 + half * (i + 1), 0:TILE] for i in parts]
        right = [x_ref[k0 + half * i : k0 + half * (i + 1), TILE:] for i in parts]
        cols = [[whole(v[:, k0 + j : k0 + j + 1]) for v in left] for j in range(BLOCK)]
        upper = [jnp.zeros((half, TILE), F32) for _ in parts]
        for j in range(BLOCK):
            f = cols[j]
            own, row = j // half, j % half
            here = sub == row
            inv = 1.0 / whole(f[own][row : row + 1, :])
            u_ref[k0 + j : k0 + j + 1, :] = right[own][row : row + 1, :]
            for i in parts:
                if i > own:
                    continue
                v = -f[i] * inv
                if i == own:
                    v = jnp.where(here, inv, jnp.where(sub < row, v, 0.0))
                upper[i] = jnp.where(lane == k0 + j, v, upper[i])

            def eliminate(v):
                pivot_row = whole(v[own][row : row + 1, :]) * inv
                rest = [v[i] - f[i] * pivot_row for i in parts]
                rest[own] = jnp.where(here, pivot_row, rest[own])
                return rest

            for jj in range(j + 1, BLOCK):
                cols[jj] = eliminate(cols[jj])
            left = eliminate(left)
            right = eliminate(right)

        def three(v):
            h, l = halves(v)
            return jnp.concatenate([h, h, l], 0)

        t = jnp.concatenate([jnp.concatenate(left, 0), jnp.concatenate(right, 0)], 1)
        prod = mm(a, three(t))
        for i in range(side // half):
            rows = slice(half * i, half * (i + 1))
            if k0 <= half * i < k0 + BLOCK:
                x_ref[rows, :] = t[half * i - k0 : half * (i + 1) - k0, :]
            else:
                x_ref[rows, :] = x_ref[rows, :] - prod[rows, :]
        v = jnp.concatenate(upper, 0)
        if k0:
            above = mm(a, three(v))
            inv_ref[0:k0, :] = inv_ref[0:k0, :] - above[0:k0, :]
        inv_ref[k0 : k0 + BLOCK, :] = v


def solve_kernel(picked, own_tab, own_side, root_tab, root_side, b_out, u_out, right, x, upper):
    is_root = lax.axis_index("col") == 0
    pk = picked[...]
    eye = (lax.broadcasted_iota(I32, (TILE, TILE), 0) == lax.broadcasted_iota(I32, (TILE, TILE), 1))
    right[:, 0:TILE] = jnp.zeros((TILE, TILE), BF)
    right[:, TILE:] = jnp.where(lax.broadcasted_iota(I32, (TILE, TILE), 0) == 24, 1.0, 0.0).astype(BF)
    x[:, 0:TILE] = pivot_block(pk, pk[4:5], root_tab, root_side, right) + jnp.where(eye, JUMP, 0.0)
    x[:, TILE:] = pivot_block(pk, pk[3:4], own_tab, own_side, right) + jnp.where(eye & is_root, JUMP, 0.0)
    factor(x, upper, u_out)
    wh, wl = halves(jnp.where(is_root, upper[...], -x[:, TILE:]))
    b_out[0:TILE, 0:TILE] = wh
    b_out[0:TILE, TILE:] = wl
    b_out[TILE:, 0:TILE] = wh
    b_out[TILE:, TILE:] = jnp.zeros_like(wl)


def apply_kernel(counts_hbm, message, b, own, rest, root, out_hbm, counts, scalars, ready, sems, out_sems, *, accs):
    tiles = root.shape[0] // TILE
    early = own.shape[0] // TILE
    loads = [
        pltpu.make_async_copy(counts_hbm, counts, sems.at[0]),
        pltpu.make_async_copy(message, scalars, sems.at[1]),
    ]
    for load in loads:
        load.start()
    keep = jnp.where(lax.axis_index("col") == 0, 0.0, 2.0)

    def out_copy(g):
        rows = pl.ds(pl.multiple_of(g * (WAYS * TILE), TILE), WAYS * TILE)
        return pltpu.make_async_copy(ready.at[rows, :], out_hbm.at[rows, :], out_sems.at[g])

    def product(*accs):
        for unit in range(2):
            pltpu.matmul_push_rhs(b[...], 0, unit)

        def begin(slot, t, first):
            h, l = halves(root[tile_rows(jnp.minimum(t, tiles - 1)), :])
            a = jnp.concatenate([h, l], 1)
            pltpu.matmul_acc_lhs(accs[slot], a, load_staged_rhs=0 if first else None)

        for slot in range(WAYS):
            begin(slot, slot, slot < 2)
        for load in loads:
            load.wait()

        def part(block, first):
            def group(g, carry):
                for slot in range(WAYS):
                    at = g * WAYS + slot
                    t = first + at
                    n0 = jnp.full((1, TILE), scalars[4, t], F32)
                    nc = jnp.full((1, TILE), counts[t], I32).astype(F32)
                    p = pltpu.matmul_pop(accs[slot])
                    prod = (p[:, 0:TILE] + p[:, TILE:]) * (2.0 / n0)
                    ready[tile_rows(t), :] = block[tile_rows(at), :] * (keep / nc) + prod
                    begin(slot, t + WAYS, False)
                out_copy(first // WAYS + g).start()
                return carry

            lax.fori_loop(0, block.shape[0] // TILE // WAYS, group, 0)

        part(own, 0)
        part(rest, early)
        for acc in accs:
            pltpu.matmul_pop(acc)

    pl.run_scoped(product, *accs[:WAYS])

    def finish(g, carry):
        out_copy(g).wait()
        return carry

    lax.fori_loop(0, tiles // WAYS, finish, 0)


def vmem():
    return pl.BlockSpec(memory_space=pltpu.VMEM)


def hbm():
    return pl.BlockSpec(memory_space=pltpu.HBM)


def numbered(send, steps):
    parts = []
    for k in steps:
        parts.append(send(k))
    return parts


def limit(mib):
    return pltpu.CompilerParams(vmem_limit_bytes=mib * 1024 * 1024)


def steps(accs, colloc_points, sources, counts, row_element, pivots):
    local_rows = colloc_points.shape[1]
    tiles = local_rows // TILE
    early = tiles // 2
    own_counts = counts.reshape(tiles)
    col = lax.axis_index("col")

    def stay(v):
        return pltpu.with_memory_space_constraint(v, pltpu.HBM)

    table = jax.ShapeDtypeStruct((2 * PAIRS + 1, FEATS, 2 * TILE), BF)
    aside = jax.ShapeDtypeStruct((FEATS, 2 * TILE), BF)

    def part(count):
        return jax.ShapeDtypeStruct((count * TILE, TILE), F32)

    wide = pltpu.VMEM((QUAD_MAX * FEATS, TILE), F32)
    message_block = jax.ShapeDtypeStruct((8, TILE), F32)
    scalar_counts = pltpu.SMEM((tiles,), I32)
    scalar_message = pltpu.SMEM((8, TILE), F32)

    message = pl.pallas_call(
        pack_kernel,
        out_shape=message_block,
        in_specs=[hbm()] * 2,
        out_specs=vmem(),
        scratch_shapes=[pltpu.VMEM((1, tiles), I32), pltpu.SemaphoreType.DMA((2,))],
        compiler_params=limit(4),
        name="pack",
    )(stay(sources), stay(own_counts.reshape(1, tiles)))
    got = numbered(lambda k: lax.ppermute(message, "col", [(0, k)]), (2, 1, 3))
    y_part = jnp.where(col == 0, message, got[0] + got[1] + got[2])
    got = numbered(lambda k: lax.ppermute(y_part, "col", [(i, i + k) for i in range(4)]), (8, 4, 12))
    root_message = jnp.where(col < 4, y_part, got[0] + got[1] + got[2])
    own_sum, lhs, own_tab, own_side, found = pl.pallas_call(
        functools.partial(own_kernel, accs=accs),
        out_shape=(part(early), jax.ShapeDtypeStruct((local_rows, TILE), BF), table, aside, message_block),
        in_specs=[hbm()] * 4 + [vmem()],
        out_specs=(vmem(),) * 5,
        scratch_shapes=[
            scalar_counts,
            pltpu.VMEM(colloc_points.shape, F32),
            pltpu.VMEM((tiles, TILE), I32),
            pltpu.VMEM((1, TILE), I32),
            wide,
            pltpu.VMEM((early * TILE, TILE), F32),
            pltpu.SemaphoreType.DMA((4,)),
        ],
        compiler_params=limit(12),
        name="own",
    )(
        stay(own_counts),
        stay(colloc_points),
        stay(row_element.reshape(tiles, TILE)),
        stay(pivots.reshape(1, TILE)),
        message,
    )
    picked = pl.pallas_call(
        pick_kernel,
        out_shape=message_block,
        in_specs=[vmem()] * 2,
        out_specs=vmem(),
        compiler_params=limit(4),
        name="pick",
    )(found, root_message)
    picked = picked + lax.ppermute(picked, "row", [(i, i ^ 1) for i in range(8)])
    got = numbered(lambda k: lax.ppermute(picked, "row", [(i, i ^ k) for i in range(8)]), (4, 2, 6))
    picked = picked + got[0] + got[1] + got[2]
    rest_sum, root_sum, root_tab, root_side = pl.pallas_call(
        functools.partial(rest_kernel, accs=accs),
        out_shape=(part(tiles - early), part(tiles), table, aside),
        in_specs=[hbm()] + [vmem()] * 4,
        out_specs=(vmem(),) * 4,
        scratch_shapes=[
            scalar_counts,
            scalar_message,
            wide,
            pltpu.VMEM((tiles * TILE, TILE), F32),
            pltpu.SemaphoreType.DMA((2,)),
        ],
        compiler_params=limit(20),
        name="rest",
    )(stay(own_counts), lhs, root_message, own_tab, own_side)
    factors, u_rows = pl.pallas_call(
        solve_kernel,
        out_shape=(
            jax.ShapeDtypeStruct((2 * TILE, 2 * TILE), BF),
            jax.ShapeDtypeStruct((TILE, TILE), F32),
        ),
        in_specs=[vmem()] * 5,
        out_specs=(vmem(), vmem()),
        scratch_shapes=[
            pltpu.VMEM((TILE, 2 * TILE), BF),
            pltpu.VMEM((TILE, 2 * TILE), F32),
            pltpu.VMEM((TILE, TILE), F32),
        ],
        compiler_params=limit(8),
        name="solve",
    )(picked, own_tab, own_side, root_tab, root_side)
    factored = pl.pallas_call(
        functools.partial(apply_kernel, accs=accs),
        out_shape=jax.ShapeDtypeStruct((local_rows, TILE), F32),
        in_specs=[hbm()] + [vmem()] * 5,
        out_specs=hbm(),
        scratch_shapes=[
            scalar_counts,
            scalar_message,
            pltpu.VMEM((local_rows, TILE), F32),
            pltpu.SemaphoreType.DMA((2,)),
            pltpu.SemaphoreType.DMA((tiles // WAYS,)),
        ],
        compiler_params=limit(20),
        name="apply",
    )(stay(own_counts), root_message, factors, own_sum, rest_sum, root_sum)
    return factored, u_rows


def body(accs, *args):
    return steps(accs, *args)


def solution(mesh):
    placed = (P(None, "row"), P(None, "col"), P("row", "col"), P("row"), P())
    with jax.sharding.use_abstract_mesh(mesh.abstract_mesh):
        accs = [pltpu.ACC(k % 2)((TILE, 2 * TILE), F32) for k in range(JOBS)]
    return jax.shard_map(
        functools.partial(body, accs),
        mesh=mesh,
        in_specs=placed,
        out_specs=(P("row", "col"), P(None, "col")),
        check_vma=False,
    )
```

```python
import functools

import jax
import jax.numpy as jnp
import numpy as np
from jax import lax
from jax.experimental import pallas as pl
from jax.experimental.pallas import tpu as pltpu
from jax.sharding import PartitionSpec as P


F32 = jnp.float32
BF = jnp.bfloat16
I32 = jnp.int32

TILE = 128
QUAD_MAX = 16
PAIRS = QUAD_MAX // 2
FEATS = 32
JUMP = 512.0
BLOCK = 16
GROUP = 10
JOBS = 8
DEPTH = 256
WAYS = 6
START = 3
FAR = 1e30


def split3(v):
    high = v.astype(BF).astype(F32)
    rest = v - high
    mid = rest.astype(BF).astype(F32)
    low = (rest - mid).astype(BF).astype(F32)
    return high, mid, low


def mm(a, b):
    return jnp.dot(a, b, preferred_element_type=F32)


def halves(v):
    high = v.astype(BF)
    return high, (v - high.astype(F32)).astype(BF)


def point_features(x, y, z, extra):
    xs = x - 0.5
    ys = y - 0.5
    rows = []
    for v in (xs, ys, z):
        h, m, l = split3(v)
        rows += [h, h, m, m, h, l]
    rows += list(split3(xs * xs + ys * ys + z * z))
    one = jnp.ones_like(x)
    rows += [one, one, one]
    rows += extra
    zero = jnp.zeros_like(x)
    rows += [zero] * (FEATS - len(rows))
    rows = jnp.concatenate(rows, 0)
    return jnp.concatenate([rows, jnp.zeros((TILE - FEATS, TILE), F32)], 0)


def quad_offsets():
    numbers = np.arange(QUAD_MAX).astype(np.float32)
    radius = np.float32(4.0) * np.sqrt((numbers + np.float32(0.5)) / np.float32(QUAD_MAX))
    angles = np.float32(2.39996323) * numbers
    return radius * np.cos(angles), radius * np.sin(angles)


def build_table(s, wide_ref, tab_ref):
    off_x, off_y = quad_offsets()
    numbers = lax.broadcasted_iota(I32, (QUAD_MAX, TILE), 0)
    ox = jnp.zeros((QUAD_MAX, TILE), F32)
    oy = ox
    for q in range(QUAD_MAX):
        ox = jnp.where(numbers == q, float(off_x[q]), ox)
        oy = jnp.where(numbers == q, float(off_y[q]), oy)
    sx, sy, sz, size = [jnp.broadcast_to(s[i : i + 1], (QUAD_MAX, TILE)) for i in range(4)]
    ux = (sx + size * ox) - 0.5
    uy = (sy + size * oy) - 0.5
    norm = ux * ux + uy * uy + sz * sz + size * size
    wide_ref[...] = jnp.zeros_like(wide_ref)

    def put(f, v):
        wide_ref[pl.ds(f, QUAD_MAX, stride=FEATS), :] = v

    for base, u in ((0, -2.0 * ux), (6, -2.0 * uy), (12, -2.0 * sz)):
        uh, um, ul = split3(u)
        for k, v in enumerate((uh, um, uh, um, ul, uh)):
            put(base + k, v)
    one = jnp.ones((QUAD_MAX, TILE), F32)
    for k in range(3):
        put(18 + k, one)
    for k, v in enumerate(split3(norm)):
        put(21 + k, v)
    for q in range(QUAD_MAX):
        columns = pl.ds(q % 2 * TILE, TILE)
        tab_ref[q // 2, :, columns] = wide_ref[pl.ds(FEATS * q, FEATS), :].astype(BF)


def depth_rows(s):
    rows = lax.broadcasted_iota(I32, (FEATS, TILE), 0)
    zh, zm, zl = split3(jnp.broadcast_to(s[2:3], (FEATS, TILE)))
    dz = jnp.where((rows == 12) | (rows == 14) | (rows == 17), 1.0, 0.0)
    dz = jnp.where(rows == 21, -zh, dz)
    dz = jnp.where(rows == 22, -zm, dz)
    return jnp.where(rows == 23, -zl, dz)


def build_side(s, first_col, side_ref):
    rows = lax.broadcasted_iota(I32, (FEATS, TILE), 0)
    ids = (lax.broadcasted_iota(I32, (FEATS, TILE), 1) + first_col).astype(F32)
    high = jnp.floor(ids * (1.0 / 256.0))
    low = ids - 256.0 * high
    e = jnp.where(rows == 24, 256.0, 0.0)
    e = jnp.where(rows == 25, 1.0, e)
    e = jnp.where(rows == 21, -256.0 * high, e)
    e = jnp.where(rows == 22, -low, e)
    side_ref[0:FEATS, 0:TILE] = depth_rows(s).astype(BF)
    side_ref[0:FEATS, TILE:] = e.astype(BF)


def tile_rows(t):
    return pl.ds(pl.multiple_of(t * TILE, TILE), TILE)


def pair_sum(p, half):
    r = lax.rsqrt(p)
    cube = r * (r * r)
    return (r[:, 0:TILE] + r[:, TILE:]) + half * (cube[:, 0:TILE] + cube[:, TILE:])


def build_lhs(points, elements, lhs):
    tiles = points.shape[1] // TILE

    def group(g, carry):
        for k in range(GROUP):
            t = g * GROUP + k
            o = pl.multiple_of(t * TILE, TILE)
            pt = points[:, pl.ds(o, TILE)]
            re = elements[pl.ds(t, 1), :].astype(F32)
            high = jnp.floor(re * (1.0 / 256.0))
            f = point_features(pt[0:1], pt[1:2], pt[2:3], [high, re - 256.0 * high])
            lhs[pl.ds(o, TILE), :] = f.T.astype(BF)
        return carry

    lax.fori_loop(0, tiles // GROUP, group, 0)


def pack_kernel(sources_hbm, counts_hbm, points_hbm, elements_hbm, pivots_hbm, out, points, elements, pivots, counts, sems):
    loads = [
        pltpu.make_async_copy(sources_hbm, out.at[pl.ds(0, 4), :], sems.at[0]),
        pltpu.make_async_copy(counts_hbm, counts, sems.at[1]),
        pltpu.make_async_copy(points_hbm, points, sems.at[2]),
        pltpu.make_async_copy(elements_hbm, elements, sems.at[3]),
        pltpu.make_async_copy(pivots_hbm, pivots, sems.at[4]),
    ]
    for load in loads:
        load.start()
    out[4:, :] = jnp.zeros((4, TILE), F32)
    for load in loads:
        load.wait()
    out[4:5, 0 : counts.shape[1]] = counts[...].astype(F32)


def tall(b, rows):
    return jnp.concatenate([b, jnp.zeros((rows - b.shape[0], b.shape[1]), BF)], 0)


def build_far(far_ref):
    lane = lax.broadcasted_iota(I32, (TILE, TILE), 1)
    far_ref[0] = jnp.zeros((TILE, TILE), BF)
    far_ref[1] = jnp.where(lane == 0, FAR, 0.0).astype(BF)
    far_ref[2] = jnp.where(lane < 2, FAR, 0.0).astype(BF)


def pair_rhs(block):
    rows = lax.broadcasted_iota(I32, (16, 2 * TILE), 0)
    lane = lax.broadcasted_iota(I32, (16, 2 * TILE), 1)
    pick = jnp.where(rows == 1 - lane // TILE, 1.0, 0.0).astype(BF)
    return jnp.concatenate([tall(block, TILE), tall(pick, DEPTH - TILE)], 0)


def assemble(count, lhs, out, weights, tab, side, depth, far, turns, sizes, first_tile, *accs):
    tiles = out.shape[0] // TILE
    none = jnp.zeros((TILE, DEPTH - TILE), BF)

    pltpu.matmul_push_rhs(tall(tab[0], DEPTH), 0, 0)
    pltpu.matmul_push_rhs(tall(side[...], DEPTH), 0, 1)

    def begin(slot, t, first):
        a = lhs[tile_rows(first_tile + jnp.minimum(t, tiles - 1)), :]
        a = jnp.concatenate([a, none], 1)
        pltpu.matmul_acc_lhs(accs[2 * slot], a, load_staged_rhs=0 if first else None)
        pltpu.matmul_acc_lhs(accs[2 * slot + 1], a, load_staged_rhs=0 if first else None)

    ways = START
    for slot in range(ways):
        begin(slot, slot, slot == 0)

    def start(g, places, last=False):
        for slot in range(ways):
            t = g * ways + slot
            p = pltpu.matmul_pop(accs[2 * slot])
            q = pltpu.matmul_pop(accs[2 * slot + 1])
            points = count(first_tile + t)
            n = jnp.full((1, TILE), points, I32).astype(F32)
            weights[pl.ds(t, 1), :] = 2.0 / n
            half = q[:, 0:TILE] * (q[:, 0:TILE] * 0.5)
            out[tile_rows(t), :] = pair_sum(p, half) + jnp.where(q[:, TILE:] == 0.0, (0.5 * JUMP) * n, 0.0)
            depth[tile_rows(t), :] = half
            if not last:
                begin(slot, t + ways, False)
            after = []
            for j in range(1, PAIRS):
                turns[j, places[j - 1]] = t
                after.append(places[j - 1] + jnp.where(points > 2 * j, 1, 0))
            places = tuple(after)
        return places

    groups = tiles // ways
    places = start(groups - 1, lax.fori_loop(0, groups - 1, start, (0,) * (PAIRS - 1)), True)
    for j in range(1, PAIRS):
        sizes[j] = places[j - 1]
    sizes[PAIRS] = 0

    def fill(j, g):
        size = sizes[j]
        b = pair_rhs(tab[jnp.minimum(j, PAIRS - 1)])
        for unit in range(2):
            pltpu.matmul_push_rhs(b, 0, unit)
        at = []
        for slot in range(JOBS):
            place = g * JOBS + slot
            t = turns[jnp.minimum(j, PAIRS - 1), jnp.maximum(jnp.minimum(place, size - 1), 0)]
            t = jnp.clip(t, 0, tiles - 1)
            points = count(first_tile + t)
            index = jnp.where(place < size, jnp.where(points > 2 * j + 1, 0, 1), 2)
            a = jnp.concatenate([lhs[tile_rows(first_tile + t), :], far[index]], 1)
            pltpu.matmul_acc_lhs(accs[slot], a, load_staged_rhs=0 if slot < 2 else None)
            at.append(t)
        more = (g + 1) * JOBS < size
        return jnp.where(more, j, jnp.minimum(j + 1, PAIRS)), jnp.where(more, g + 1, 0), tuple(at)

    def jobs(state):
        _, j, g, at = state
        busy = sizes[j]
        for slot in range(JOBS):
            rows = tile_rows(at[slot])
            p = pltpu.matmul_pop(accs[slot])
            out[rows, :] = out[rows, :] + pair_sum(p, depth[rows, :])
        return (busy,) + fill(j, g)

    lax.while_loop(lambda state: state[0] > 0, jobs, (sizes[1],) + fill(1, 0))
    for acc in accs:
        pltpu.matmul_pop(acc)


def own_kernel(counts_hbm, points, elements, pivots, message, out, weights, lhs, tab, side, found,
               counts, wide, depth, far, turns, sizes, sem, *, accs):
    load = pltpu.make_async_copy(counts_hbm, counts, sem)
    load.start()
    s = message[0:4]
    build_table(s, wide, tab)
    build_side(s, lax.axis_index("col") * TILE, side)
    build_far(far)
    build_lhs(points, elements, lhs)
    find_pivots(points, pivots, message, found)
    load.wait()
    lists = (depth, far, turns, sizes)

    @pl.when(lax.axis_index("col") != 0)
    def _():
        pl.run_scoped(functools.partial(assemble, lambda t: counts[t], lhs, out, weights, tab, side, *lists, 0), *accs)


def rest_kernel(counts_hbm, lhs, message, own_tab, own_side, rest_out, rest_weights, root_out, root_weights, tab, side,
                counts, scalars, wide, depth, far, turns, sizes, sems, *, accs):
    loads = [
        pltpu.make_async_copy(counts_hbm, counts, sems.at[0]),
        pltpu.make_async_copy(message, scalars, sems.at[1]),
    ]
    for load in loads:
        load.start()
    build_far(far)
    s = message[0:4]
    build_table(s, wide, tab)
    build_side(s, 0, side)
    for load in loads:
        load.wait()
    early = (lhs.shape[0] - rest_out.shape[0]) // TILE

    def both(*accs):
        lists = (depth, far, turns, sizes)

        @pl.when(lax.axis_index("col") != 0)
        def _():
            assemble(lambda t: counts[t], lhs, rest_out, rest_weights, own_tab, own_side, *lists, early, *accs)

        assemble(lambda t: scalars[4, t].astype(I32), lhs, root_out, root_weights, tab, side, *lists, 0, *accs)

    pl.run_scoped(both, *accs)


def find_pivots(points, pivots, message, out):
    tiles = points.shape[1] // TILE
    piv = jnp.broadcast_to(pivots[...], (8, TILE))
    tile = jnp.right_shift(piv, 7) - lax.axis_index("row") * tiles
    lane = jnp.bitwise_and(piv, TILE - 1)
    inside = (tile >= 0) & (tile < tiles)
    found = jnp.zeros((8, TILE), F32)
    for t in range(tiles):
        pt = jnp.concatenate([points[:, t * TILE : (t + 1) * TILE], jnp.zeros((5, TILE), F32)], 0)
        got = jnp.take_along_axis(pt, lane, axis=1, mode="promise_in_bounds")
        found = jnp.where(tile == t, got, found)
    at = jnp.clip(tile, 0, tiles - 1)
    count = jnp.take_along_axis(message[...], at, axis=1, mode="promise_in_bounds")
    rows = lax.broadcasted_iota(I32, (8, TILE), 0)
    found = jnp.where((rows == 3) & inside, jnp.broadcast_to(count[4:5], (8, TILE)), found)
    out[...] = jnp.where((rows == 4) & inside, (tile + 1).astype(F32), found)


def pick_kernel(found, root, out):
    tile = jnp.broadcast_to(found[4:5], (8, TILE))
    at = jnp.maximum(tile.astype(I32) - 1, 0)
    count = jnp.take_along_axis(root[...], at, axis=1, mode="promise_in_bounds")
    rows = lax.broadcasted_iota(I32, (8, TILE), 0)
    count = jnp.where(tile > 0.0, jnp.broadcast_to(count[4:5], (8, TILE)), 0.0)
    out[...] = jnp.where(rows == 4, count, found[...])


def pivot_block(points, n_row, tab, side, right):
    f = point_features(points[0:1], points[1:2], points[2:3], [n_row])
    numbers = lax.broadcasted_iota(I32, (QUAD_MAX, TILE), 0)
    absent = jnp.where(numbers.astype(F32) >= n_row, FAR, 0.0)
    f = jnp.concatenate([f[0:FEATS], absent, f[FEATS + QUAD_MAX :]], 0)
    a = f.T.astype(BF)
    right[0:FEATS, 0:TILE] = side[:, 0:TILE]
    q = mm(a, right[...])
    half = q[:, 0:TILE] * (q[:, 0:TILE] * 0.5)
    numbers = lax.broadcasted_iota(I32, (QUAD_MAX, 2 * TILE), 0) - lax.broadcasted_iota(I32, (QUAD_MAX, 2 * TILE), 1) // TILE
    total = jnp.zeros((TILE, TILE), F32)
    for j in range(PAIRS):
        pick = jnp.where(numbers == 2 * j, 1.0, 0.0).astype(BF)
        total = total + pair_sum(mm(a, tall(jnp.concatenate([tab[j], pick], 0), TILE)), half)
    return total * (2.0 / q[:, TILE:])


def factor(x_ref, inv_ref, u_ref):
    side = TILE
    half = 8
    sub = lax.broadcasted_iota(I32, (half, TILE), 0)
    lane = lax.broadcasted_iota(I32, (half, TILE), 1)
    big = lax.broadcasted_iota(I32, (side, TILE), 0)
    inv_ref[...] = jnp.zeros_like(inv_ref)
    parts = range(BLOCK // half)

    def whole(rows):
        return jnp.broadcast_to(rows, (half, TILE))

    for b in range(side // BLOCK):
        k0 = b * BLOCK
        block = x_ref[:, k0 : k0 + BLOCK]
        high = block.astype(BF).astype(F32)
        a = jnp.concatenate([high, block - high, high], 1).astype(BF)
        left = [x_ref[k0 + half * i : k0 + half * (i + 1), 0:TILE] for i in parts]
        right = [x_ref[k0 + half * i : k0 + half * (i + 1), TILE:] for i in parts]
        cols = [[whole(v[:, k0 + j : k0 + j + 1]) for v in left] for j in range(BLOCK)]
        upper = [jnp.zeros((half, TILE), F32) for _ in parts]
        for j in range(BLOCK):
            f = cols[j]
            own, row = j // half, j % half
            here = sub == row
            inv = 1.0 / whole(f[own][row : row + 1, :])
            u_ref[k0 + j : k0 + j + 1, :] = right[own][row : row + 1, :]
            for i in parts:
                if i > own:
                    continue
                v = -f[i] * inv
                if i == own:
                    v = jnp.where(here, inv, jnp.where(sub < row, v, 0.0))
                upper[i] = jnp.where(lane == k0 + j, v, upper[i])

            def eliminate(v):
                pivot_row = whole(v[own][row : row + 1, :]) * inv
                rest = [v[i] - f[i] * pivot_row for i in parts]
                rest[own] = jnp.where(here, pivot_row, rest[own])
                return rest

            for jj in range(j + 1, BLOCK):
                cols[jj] = eliminate(cols[jj])
            left = eliminate(left)
            right = eliminate(right)

        def three(v):
            h, l = halves(v)
            return jnp.concatenate([h, h, l], 0)

        t = jnp.concatenate([jnp.concatenate(left, 0), jnp.concatenate(right, 0)], 1)
        prod = mm(a, three(t))
        for i in range(side // half):
            rows = slice(half * i, half * (i + 1))
            if k0 <= half * i < k0 + BLOCK:
                x_ref[rows, :] = t[half * i - k0 : half * (i + 1) - k0, :]
            else:
                x_ref[rows, :] = x_ref[rows, :] - prod[rows, :]
        v = jnp.concatenate(upper, 0)
        if k0:
            above = mm(a, three(v))
            inv_ref[0:k0, :] = inv_ref[0:k0, :] - above[0:k0, :]
        inv_ref[k0 : k0 + BLOCK, :] = v


def solve_kernel(picked, own_tab, own_side, root_tab, root_side, b_out, u_out, right, x, upper):
    is_root = lax.axis_index("col") == 0
    pk = picked[...]
    eye = (lax.broadcasted_iota(I32, (TILE, TILE), 0) == lax.broadcasted_iota(I32, (TILE, TILE), 1))
    right[:, 0:TILE] = jnp.zeros((TILE, TILE), BF)
    right[:, TILE:] = jnp.where(lax.broadcasted_iota(I32, (TILE, TILE), 0) == 24, 1.0, 0.0).astype(BF)
    x[:, 0:TILE] = pivot_block(pk, pk[4:5], root_tab, root_side, right) + jnp.where(eye, JUMP, 0.0)
    x[:, TILE:] = pivot_block(pk, pk[3:4], own_tab, own_side, right) + jnp.where(eye & is_root, JUMP, 0.0)
    factor(x, upper, u_out)
    wh, wl = halves(jnp.where(is_root, upper[...], -x[:, TILE:]))
    b_out[0:TILE, 0:TILE] = wh
    b_out[0:TILE, TILE:] = wl
    b_out[TILE:, 0:TILE] = wh
    b_out[TILE:, TILE:] = jnp.zeros_like(wl)


def apply_kernel(b, own, own_weights, rest, rest_weights, root, root_weights, out_hbm, ready, out_sems, *, accs):
    tiles = root.shape[0] // TILE
    early = own.shape[0] // TILE
    is_root = lax.axis_index("col") == 0

    def out_copy(g):
        rows = pl.ds(pl.multiple_of(g * (WAYS * TILE), TILE), WAYS * TILE)
        return pltpu.make_async_copy(ready.at[rows, :], out_hbm.at[rows, :], out_sems.at[g])

    def product(*accs):
        for unit in range(2):
            pltpu.matmul_push_rhs(b[...], 0, unit)

        def begin(slot, t, first):
            h, l = halves(root[tile_rows(jnp.minimum(t, tiles - 1)), :])
            a = jnp.concatenate([h, l], 1)
            pltpu.matmul_acc_lhs(accs[slot], a, load_staged_rhs=0 if first else None)

        for slot in range(WAYS):
            begin(slot, slot, slot < 2)

        def part(block, weights, first):
            def group(g, carry):
                for slot in range(WAYS):
                    at = g * WAYS + slot
                    t = first + at
                    p = pltpu.matmul_pop(accs[slot])
                    prod = (p[:, 0:TILE] + p[:, TILE:]) * root_weights[pl.ds(t, 1), :]
                    base = jnp.where(is_root, 0.0, block[tile_rows(at), :] * weights[pl.ds(at, 1), :])
                    ready[tile_rows(t), :] = base + prod
                    begin(slot, t + WAYS, False)
                out_copy(first // WAYS + g).start()
                return carry

            lax.fori_loop(0, block.shape[0] // TILE // WAYS, group, 0)

        part(own, own_weights, 0)
        part(rest, rest_weights, early)
        for acc in accs:
            pltpu.matmul_pop(acc)

    pl.run_scoped(product, *accs[:WAYS])

    def finish(g, carry):
        out_copy(g).wait()
        return carry

    lax.fori_loop(0, tiles // WAYS, finish, 0)


def vmem():
    return pl.BlockSpec(memory_space=pltpu.VMEM)


def hbm():
    return pl.BlockSpec(memory_space=pltpu.HBM)


def numbered(send, steps):
    parts = []
    for k in steps:
        parts.append(send(k))
    return parts


def limit(mib):
    return pltpu.CompilerParams(vmem_limit_bytes=mib * 1024 * 1024)


def steps(accs, colloc_points, sources, counts, row_element, pivots):
    local_rows = colloc_points.shape[1]
    tiles = local_rows // TILE
    early = tiles // 2
    own_counts = counts.reshape(tiles)
    col = lax.axis_index("col")

    def stay(v):
        return pltpu.with_memory_space_constraint(v, pltpu.HBM)

    table = jax.ShapeDtypeStruct((PAIRS, FEATS, 2 * TILE), BF)
    aside = jax.ShapeDtypeStruct((FEATS, 2 * TILE), BF)

    def part(count):
        return jax.ShapeDtypeStruct((count * TILE, TILE), F32)

    def rows(count):
        return jax.ShapeDtypeStruct((count, TILE), F32)

    wide = pltpu.VMEM((QUAD_MAX * FEATS, TILE), F32)
    message_block = jax.ShapeDtypeStruct((8, TILE), F32)
    scalar_counts = pltpu.SMEM((tiles,), I32)
    scalar_message = pltpu.SMEM((8, TILE), F32)
    lists = [pltpu.VMEM((3, TILE, TILE), BF), pltpu.SMEM((PAIRS, tiles + 1), I32), pltpu.SMEM((PAIRS + 1,), I32)]

    message, points, elements, pivot_row = pl.pallas_call(
        pack_kernel,
        out_shape=(
            message_block,
            jax.ShapeDtypeStruct(colloc_points.shape, F32),
            jax.ShapeDtypeStruct((tiles, TILE), I32),
            jax.ShapeDtypeStruct((1, TILE), I32),
        ),
        in_specs=[hbm()] * 5,
        out_specs=(vmem(),) * 4,
        scratch_shapes=[pltpu.VMEM((1, tiles), I32), pltpu.SemaphoreType.DMA((5,))],
        compiler_params=limit(4),
        name="pack",
    )(
        stay(sources),
        stay(own_counts.reshape(1, tiles)),
        stay(colloc_points),
        stay(row_element.reshape(tiles, TILE)),
        stay(pivots.reshape(1, TILE)),
    )
    got = numbered(lambda k: lax.ppermute(message, "col", [(0, k)]), (2, 3, 1))
    y_part = jnp.where(col == 0, message, got[0] + got[1] + got[2])
    got = numbered(lambda k: lax.ppermute(y_part, "col", [(i, i + k) for i in range(4)]), (8, 12, 4))
    root_message = jnp.where(col < 4, y_part, got[0] + got[1] + got[2])
    own_sum, own_weights, lhs, own_tab, own_side, found = pl.pallas_call(
        functools.partial(own_kernel, accs=accs),
        out_shape=(part(early), rows(early), jax.ShapeDtypeStruct((local_rows, TILE), BF), table, aside, message_block),
        in_specs=[hbm()] + [vmem()] * 4,
        out_specs=(vmem(),) * 6,
        scratch_shapes=[scalar_counts, wide, pltpu.VMEM((early * TILE, TILE), F32), *lists, pltpu.SemaphoreType.DMA],
        compiler_params=limit(12),
        name="own",
    )(stay(own_counts), points, elements, pivot_row, message)
    picked = pl.pallas_call(
        pick_kernel,
        out_shape=message_block,
        in_specs=[vmem()] * 2,
        out_specs=vmem(),
        compiler_params=limit(4),
        name="pick",
    )(found, root_message)
    picked = picked + lax.ppermute(picked, "row", [(i, i ^ 1) for i in range(8)])
    got = numbered(lambda k: lax.ppermute(picked, "row", [(i, i ^ k) for i in range(8)]), (4, 2, 6))
    picked = picked + got[0] + got[1] + got[2]
    rest_sum, rest_weights, root_sum, root_weights, root_tab, root_side = pl.pallas_call(
        functools.partial(rest_kernel, accs=accs),
        out_shape=(part(tiles - early), rows(tiles - early), part(tiles), rows(tiles), table, aside),
        in_specs=[hbm()] + [vmem()] * 4,
        out_specs=(vmem(),) * 6,
        scratch_shapes=[
            scalar_counts,
            scalar_message,
            wide,
            pltpu.VMEM((tiles * TILE, TILE), F32),
            *lists,
            pltpu.SemaphoreType.DMA((2,)),
        ],
        compiler_params=limit(20),
        name="rest",
    )(stay(own_counts), lhs, root_message, own_tab, own_side)
    factors, u_rows = pl.pallas_call(
        solve_kernel,
        out_shape=(
            jax.ShapeDtypeStruct((2 * TILE, 2 * TILE), BF),
            jax.ShapeDtypeStruct((TILE, TILE), F32),
        ),
        in_specs=[vmem()] * 5,
        out_specs=(vmem(), vmem()),
        scratch_shapes=[
            pltpu.VMEM((TILE, 2 * TILE), BF),
            pltpu.VMEM((TILE, 2 * TILE), F32),
            pltpu.VMEM((TILE, TILE), F32),
        ],
        compiler_params=limit(8),
        name="solve",
    )(picked, own_tab, own_side, root_tab, root_side)
    factored = pl.pallas_call(
        functools.partial(apply_kernel, accs=accs),
        out_shape=jax.ShapeDtypeStruct((local_rows, TILE), F32),
        in_specs=[vmem()] * 7,
        out_specs=hbm(),
        scratch_shapes=[pltpu.VMEM((local_rows, TILE), F32), pltpu.SemaphoreType.DMA((tiles // WAYS,))],
        compiler_params=limit(20),
        name="apply",
    )(factors, own_sum, own_weights, rest_sum, rest_weights, root_sum, root_weights)
    return factored, u_rows


def body(accs, *args):
    return steps(accs, *args)


def solution(mesh):
    placed = (P(None, "row"), P(None, "col"), P("row", "col"), P("row"), P())
    with jax.sharding.use_abstract_mesh(mesh.abstract_mesh):
        accs = [pltpu.ACC(k % 2)((TILE, 2 * TILE), F32) for k in range(JOBS)]
    return jax.shard_map(
        functools.partial(body, accs),
        mesh=mesh,
        in_specs=placed,
        out_specs=(P("row", "col"), P(None, "col")),
        check_vma=False,
    )
```

```python
import functools

import jax
import jax.numpy as jnp
import numpy as np
from jax import lax
from jax.experimental import pallas as pl
from jax.experimental.pallas import tpu as pltpu
from jax.sharding import PartitionSpec as P


F32 = jnp.float32
BF = jnp.bfloat16
I32 = jnp.int32

TILE = 128
QUAD_MAX = 16
PAIRS = QUAD_MAX // 2
FEATS = 32
JUMP = 512.0
BLOCK = 16
GROUP = 10
JOBS = 6
DEPTH = 256
WAYS = 6
START = 3
FAR = 1e30


def split3(v):
    high = v.astype(BF).astype(F32)
    rest = v - high
    mid = rest.astype(BF).astype(F32)
    low = (rest - mid).astype(BF).astype(F32)
    return high, mid, low


def mm(a, b):
    return jnp.dot(a, b, preferred_element_type=F32)


def halves(v):
    high = v.astype(BF)
    return high, (v - high.astype(F32)).astype(BF)


def point_features(x, y, z, extra):
    xs = x - 0.5
    ys = y - 0.5
    rows = []
    for v in (xs, ys, z):
        h, m, l = split3(v)
        rows += [h, h, m, m, h, l]
    rows += list(split3(xs * xs + ys * ys + z * z))
    one = jnp.ones_like(x)
    rows += [one, one, one]
    rows += extra
    zero = jnp.zeros_like(x)
    rows += [zero] * (FEATS - len(rows))
    rows = jnp.concatenate(rows, 0)
    return jnp.concatenate([rows, jnp.zeros((TILE - FEATS, TILE), F32)], 0)


def quad_offsets():
    numbers = np.arange(QUAD_MAX).astype(np.float32)
    radius = np.float32(4.0) * np.sqrt((numbers + np.float32(0.5)) / np.float32(QUAD_MAX))
    angles = np.float32(2.39996323) * numbers
    return radius * np.cos(angles), radius * np.sin(angles)


def build_table(s, wide_ref, tab_ref):
    off_x, off_y = quad_offsets()
    numbers = lax.broadcasted_iota(I32, (QUAD_MAX, TILE), 0)
    ox = jnp.zeros((QUAD_MAX, TILE), F32)
    oy = ox
    for q in range(QUAD_MAX):
        ox = jnp.where(numbers == q, float(off_x[q]), ox)
        oy = jnp.where(numbers == q, float(off_y[q]), oy)
    sx, sy, sz, size = [jnp.broadcast_to(s[i : i + 1], (QUAD_MAX, TILE)) for i in range(4)]
    ux = (sx + size * ox) - 0.5
    uy = (sy + size * oy) - 0.5
    norm = ux * ux + uy * uy + sz * sz + size * size
    wide_ref[...] = jnp.zeros_like(wide_ref)

    def put(f, v):
        wide_ref[pl.ds(f, QUAD_MAX, stride=FEATS), :] = v

    for base, u in ((0, -2.0 * ux), (6, -2.0 * uy), (12, -2.0 * sz)):
        uh, um, ul = split3(u)
        for k, v in enumerate((uh, um, uh, um, ul, uh)):
            put(base + k, v)
    one = jnp.ones((QUAD_MAX, TILE), F32)
    for k in range(3):
        put(18 + k, one)
    for k, v in enumerate(split3(norm)):
        put(21 + k, v)
    for q in range(QUAD_MAX):
        columns = pl.ds(q % 2 * TILE, TILE)
        tab_ref[q // 2, :, columns] = wide_ref[pl.ds(FEATS * q, FEATS), :].astype(BF)


def depth_rows(s):
    rows = lax.broadcasted_iota(I32, (FEATS, TILE), 0)
    zh, zm, zl = split3(jnp.broadcast_to(s[2:3], (FEATS, TILE)))
    dz = jnp.where((rows == 12) | (rows == 14) | (rows == 17), 1.0, 0.0)
    dz = jnp.where(rows == 21, -zh, dz)
    dz = jnp.where(rows == 22, -zm, dz)
    return jnp.where(rows == 23, -zl, dz)


def build_side(s, first_col, side_ref):
    rows = lax.broadcasted_iota(I32, (FEATS, TILE), 0)
    ids = (lax.broadcasted_iota(I32, (FEATS, TILE), 1) + first_col).astype(F32)
    high = jnp.floor(ids * (1.0 / 256.0))
    low = ids - 256.0 * high
    e = jnp.where(rows == 24, 256.0, 0.0)
    e = jnp.where(rows == 25, 1.0, e)
    e = jnp.where(rows == 21, -256.0 * high, e)
    e = jnp.where(rows == 22, -low, e)
    side_ref[0:FEATS, 0:TILE] = depth_rows(s).astype(BF)
    side_ref[0:FEATS, TILE:] = e.astype(BF)


def tile_rows(t):
    return pl.ds(pl.multiple_of(t * TILE, TILE), TILE)


def pair_sum(p, half):
    r = lax.rsqrt(p)
    cube = r * (r * r)
    return (r[:, 0:TILE] + r[:, TILE:]) + half * (cube[:, 0:TILE] + cube[:, TILE:])


def build_lhs(points, elements, lhs):
    tiles = points.shape[1] // TILE

    def group(g, carry):
        for k in range(GROUP):
            t = g * GROUP + k
            o = pl.multiple_of(t * TILE, TILE)
            pt = points[:, pl.ds(o, TILE)]
            re = elements[pl.ds(t, 1), :].astype(F32)
            high = jnp.floor(re * (1.0 / 256.0))
            f = point_features(pt[0:1], pt[1:2], pt[2:3], [high, re - 256.0 * high])
            lhs[pl.ds(o, TILE), :] = f.T.astype(BF)
        return carry

    lax.fori_loop(0, tiles // GROUP, group, 0)


def pack_kernel(sources_hbm, counts_hbm, points_hbm, elements_hbm, pivots_hbm, out, points, elements, pivots, counts, sems):
    loads = [
        pltpu.make_async_copy(sources_hbm, out.at[pl.ds(0, 4), :], sems.at[0]),
        pltpu.make_async_copy(counts_hbm, counts, sems.at[1]),
        pltpu.make_async_copy(points_hbm, points, sems.at[2]),
        pltpu.make_async_copy(elements_hbm, elements, sems.at[3]),
        pltpu.make_async_copy(pivots_hbm, pivots, sems.at[4]),
    ]
    for load in loads:
        load.start()
    out[4:, :] = jnp.zeros((4, TILE), F32)
    for load in loads:
        load.wait()
    out[4:5, 0 : counts.shape[1]] = counts[...].astype(F32)


def tall(b, rows):
    return jnp.concatenate([b, jnp.zeros((rows - b.shape[0], b.shape[1]), BF)], 0)


def build_far(far_ref):
    lane = lax.broadcasted_iota(I32, (TILE, TILE), 1)
    far_ref[0] = jnp.zeros((TILE, TILE), BF)
    far_ref[1] = jnp.where(lane == 0, FAR, 0.0).astype(BF)
    far_ref[2] = jnp.where(lane < 2, FAR, 0.0).astype(BF)


def pair_rhs(block):
    rows = lax.broadcasted_iota(I32, (16, 2 * TILE), 0)
    lane = lax.broadcasted_iota(I32, (16, 2 * TILE), 1)
    pick = jnp.where(rows == 1 - lane // TILE, 1.0, 0.0).astype(BF)
    return jnp.concatenate([tall(block, TILE), tall(pick, DEPTH - TILE)], 0)


def assemble(count, lhs, out, weights, tab, side, depth, far, turns, sizes, first_tile, *accs):
    tiles = out.shape[0] // TILE
    none = jnp.zeros((TILE, DEPTH - TILE), BF)

    pltpu.matmul_push_rhs(tall(tab[0], DEPTH), 0, 0)
    pltpu.matmul_push_rhs(tall(side[...], DEPTH), 0, 1)

    def begin(slot, t, first):
        a = lhs[tile_rows(first_tile + jnp.minimum(t, tiles - 1)), :]
        a = jnp.concatenate([a, none], 1)
        pltpu.matmul_acc_lhs(accs[2 * slot], a, load_staged_rhs=0 if first else None)
        pltpu.matmul_acc_lhs(accs[2 * slot + 1], a, load_staged_rhs=0 if first else None)

    ways = START
    for slot in range(ways):
        begin(slot, slot, slot == 0)

    def start(g, places, last=False):
        for slot in range(ways):
            t = g * ways + slot
            p = pltpu.matmul_pop(accs[2 * slot])
            q = pltpu.matmul_pop(accs[2 * slot + 1])
            points = count(first_tile + t)
            n = jnp.full((1, TILE), points, I32).astype(F32)
            weights[pl.ds(t, 1), :] = 2.0 / n
            half = q[:, 0:TILE] * (q[:, 0:TILE] * 0.5)
            out[tile_rows(t), :] = pair_sum(p, half) + jnp.where(q[:, TILE:] == 0.0, (0.5 * JUMP) * n, 0.0)
            depth[tile_rows(t), :] = half
            if not last:
                begin(slot, t + ways, False)
            after = []
            for j in range(1, PAIRS):
                turns[j, places[j - 1]] = t
                after.append(places[j - 1] + jnp.where(points > 2 * j, 1, 0))
            places = tuple(after)
        return places

    groups = tiles // ways
    places = start(groups - 1, lax.fori_loop(0, groups - 1, start, (0,) * (PAIRS - 1)), True)
    for j in range(1, PAIRS):
        sizes[j] = places[j - 1]
    sizes[PAIRS] = 0

    def fill(j, g):
        size = sizes[j]
        b = pair_rhs(tab[jnp.minimum(j, PAIRS - 1)])
        for unit in range(2):
            pltpu.matmul_push_rhs(b, 0, unit)
        at = []
        for slot in range(JOBS):
            place = g * JOBS + slot
            t = turns[jnp.minimum(j, PAIRS - 1), jnp.maximum(jnp.minimum(place, size - 1), 0)]
            t = jnp.clip(t, 0, tiles - 1)
            points = count(first_tile + t)
            index = jnp.where(place < size, jnp.where(points > 2 * j + 1, 0, 1), 2)
            a = jnp.concatenate([lhs[tile_rows(first_tile + t), :], far[index]], 1)
            pltpu.matmul_acc_lhs(accs[slot], a, load_staged_rhs=0 if slot < 2 else None)
            at.append(t)
        more = (g + 1) * JOBS < size
        return jnp.where(more, j, jnp.minimum(j + 1, PAIRS)), jnp.where(more, g + 1, 0), tuple(at)

    def jobs(state):
        _, j, g, at = state
        busy = sizes[j]
        for slot in range(JOBS):
            rows = tile_rows(at[slot])
            p = pltpu.matmul_pop(accs[slot])
            out[rows, :] = out[rows, :] + pair_sum(p, depth[rows, :])
        return (busy,) + fill(j, g)

    lax.while_loop(lambda state: state[0] > 0, jobs, (sizes[1],) + fill(1, 0))
    for acc in accs:
        pltpu.matmul_pop(acc)


def own_kernel(counts_hbm, points, elements, pivots, message, out, weights, lhs, tab, side, found,
               counts, wide, depth, far, turns, sizes, sem, *, accs):
    load = pltpu.make_async_copy(counts_hbm, counts, sem)
    load.start()
    s = message[0:4]
    build_table(s, wide, tab)
    build_side(s, lax.axis_index("col") * TILE, side)
    build_far(far)
    build_lhs(points, elements, lhs)
    find_pivots(points, pivots, message, found)
    load.wait()
    lists = (depth, far, turns, sizes)

    @pl.when(lax.axis_index("col") != 0)
    def _():
        pl.run_scoped(functools.partial(assemble, lambda t: counts[t], lhs, out, weights, tab, side, *lists, 0), *accs)


def rest_kernel(counts_hbm, lhs, message, own_tab, own_side, rest_out, rest_weights, root_out, root_weights, tab, side,
                counts, scalars, wide, depth, far, turns, sizes, sems, *, accs):
    loads = [
        pltpu.make_async_copy(counts_hbm, counts, sems.at[0]),
        pltpu.make_async_copy(message, scalars, sems.at[1]),
    ]
    for load in loads:
        load.start()
    build_far(far)
    s = message[0:4]
    build_table(s, wide, tab)
    build_side(s, 0, side)
    for load in loads:
        load.wait()
    early = (lhs.shape[0] - rest_out.shape[0]) // TILE

    def both(*accs):
        lists = (depth, far, turns, sizes)

        @pl.when(lax.axis_index("col") != 0)
        def _():
            assemble(lambda t: counts[t], lhs, rest_out, rest_weights, own_tab, own_side, *lists, early, *accs)

        assemble(lambda t: scalars[4, t].astype(I32), lhs, root_out, root_weights, tab, side, *lists, 0, *accs)

    pl.run_scoped(both, *accs)


def find_pivots(points, pivots, message, out):
    tiles = points.shape[1] // TILE
    piv = jnp.broadcast_to(pivots[...], (8, TILE))
    tile = jnp.right_shift(piv, 7) - lax.axis_index("row") * tiles
    lane = jnp.bitwise_and(piv, TILE - 1)
    inside = (tile >= 0) & (tile < tiles)
    found = jnp.zeros((8, TILE), F32)
    for t in range(tiles):
        pt = jnp.concatenate([points[:, t * TILE : (t + 1) * TILE], jnp.zeros((5, TILE), F32)], 0)
        got = jnp.take_along_axis(pt, lane, axis=1, mode="promise_in_bounds")
        found = jnp.where(tile == t, got, found)
    at = jnp.clip(tile, 0, tiles - 1)
    count = jnp.take_along_axis(message[...], at, axis=1, mode="promise_in_bounds")
    rows = lax.broadcasted_iota(I32, (8, TILE), 0)
    found = jnp.where((rows == 3) & inside, jnp.broadcast_to(count[4:5], (8, TILE)), found)
    out[...] = jnp.where((rows == 4) & inside, (tile + 1).astype(F32), found)


def pick_kernel(found, root, out):
    tile = jnp.broadcast_to(found[4:5], (8, TILE))
    at = jnp.maximum(tile.astype(I32) - 1, 0)
    count = jnp.take_along_axis(root[...], at, axis=1, mode="promise_in_bounds")
    rows = lax.broadcasted_iota(I32, (8, TILE), 0)
    count = jnp.where(tile > 0.0, jnp.broadcast_to(count[4:5], (8, TILE)), 0.0)
    out[...] = jnp.where(rows == 4, count, found[...])


def pivot_block(points, n_row, tab, side, right):
    f = point_features(points[0:1], points[1:2], points[2:3], [n_row])
    numbers = lax.broadcasted_iota(I32, (QUAD_MAX, TILE), 0)
    absent = jnp.where(numbers.astype(F32) >= n_row, FAR, 0.0)
    f = jnp.concatenate([f[0:FEATS], absent, f[FEATS + QUAD_MAX :]], 0)
    a = f.T.astype(BF)
    right[0:FEATS, 0:TILE] = side[:, 0:TILE]
    q = mm(a, right[...])
    half = q[:, 0:TILE] * (q[:, 0:TILE] * 0.5)
    numbers = lax.broadcasted_iota(I32, (QUAD_MAX, 2 * TILE), 0) - lax.broadcasted_iota(I32, (QUAD_MAX, 2 * TILE), 1) // TILE
    total = jnp.zeros((TILE, TILE), F32)
    for j in range(PAIRS):
        pick = jnp.where(numbers == 2 * j, 1.0, 0.0).astype(BF)
        total = total + pair_sum(mm(a, tall(jnp.concatenate([tab[j], pick], 0), TILE)), half)
    return total * (2.0 / q[:, TILE:])


def factor(x_ref, inv_ref, u_ref):
    side = TILE
    half = 8
    sub = lax.broadcasted_iota(I32, (half, TILE), 0)
    lane = lax.broadcasted_iota(I32, (half, TILE), 1)
    big = lax.broadcasted_iota(I32, (side, TILE), 0)
    inv_ref[...] = jnp.zeros_like(inv_ref)
    parts = range(BLOCK // half)

    def whole(rows):
        return jnp.broadcast_to(rows, (half, TILE))

    for b in range(side // BLOCK):
        k0 = b * BLOCK
        block = x_ref[:, k0 : k0 + BLOCK]
        high = block.astype(BF).astype(F32)
        a = jnp.concatenate([high, block - high, high], 1).astype(BF)
        left = [x_ref[k0 + half * i : k0 + half * (i + 1), 0:TILE] for i in parts]
        right = [x_ref[k0 + half * i : k0 + half * (i + 1), TILE:] for i in parts]
        cols = [[whole(v[:, k0 + j : k0 + j + 1]) for v in left] for j in range(BLOCK)]
        upper = [jnp.zeros((half, TILE), F32) for _ in parts]
        for j in range(BLOCK):
            f = cols[j]
            own, row = j // half, j % half
            here = sub == row
            inv = 1.0 / whole(f[own][row : row + 1, :])
            u_ref[k0 + j : k0 + j + 1, :] = right[own][row : row + 1, :]
            for i in parts:
                if i > own:
                    continue
                v = -f[i] * inv
                if i == own:
                    v = jnp.where(here, inv, jnp.where(sub < row, v, 0.0))
                upper[i] = jnp.where(lane == k0 + j, v, upper[i])

            def eliminate(v):
                pivot_row = whole(v[own][row : row + 1, :]) * inv
                rest = [v[i] - f[i] * pivot_row for i in parts]
                rest[own] = jnp.where(here, pivot_row, rest[own])
                return rest

            for jj in range(j + 1, BLOCK):
                cols[jj] = eliminate(cols[jj])
            left = eliminate(left)
            right = eliminate(right)

        def three(v):
            h, l = halves(v)
            return jnp.concatenate([h, h, l], 0)

        t = jnp.concatenate([jnp.concatenate(left, 0), jnp.concatenate(right, 0)], 1)
        prod = mm(a, three(t))
        for i in range(side // half):
            rows = slice(half * i, half * (i + 1))
            if k0 <= half * i < k0 + BLOCK:
                x_ref[rows, :] = t[half * i - k0 : half * (i + 1) - k0, :]
            else:
                x_ref[rows, :] = x_ref[rows, :] - prod[rows, :]
        v = jnp.concatenate(upper, 0)
        if k0:
            above = mm(a, three(v))
            inv_ref[0:k0, :] = inv_ref[0:k0, :] - above[0:k0, :]
        inv_ref[k0 : k0 + BLOCK, :] = v


def solve_kernel(picked, own_tab, own_side, root_tab, root_side, b_out, u_out, right, x, upper):
    is_root = lax.axis_index("col") == 0
    pk = picked[...]
    eye = (lax.broadcasted_iota(I32, (TILE, TILE), 0) == lax.broadcasted_iota(I32, (TILE, TILE), 1))
    right[:, 0:TILE] = jnp.zeros((TILE, TILE), BF)
    right[:, TILE:] = jnp.where(lax.broadcasted_iota(I32, (TILE, TILE), 0) == 24, 1.0, 0.0).astype(BF)
    x[:, 0:TILE] = pivot_block(pk, pk[4:5], root_tab, root_side, right) + jnp.where(eye, JUMP, 0.0)
    x[:, TILE:] = pivot_block(pk, pk[3:4], own_tab, own_side, right) + jnp.where(eye & is_root, JUMP, 0.0)
    factor(x, upper, u_out)
    wh, wl = halves(jnp.where(is_root, upper[...], -x[:, TILE:]))
    b_out[0:TILE, 0:TILE] = wh
    b_out[0:TILE, TILE:] = wl
    b_out[TILE:, 0:TILE] = wh
    b_out[TILE:, TILE:] = jnp.zeros_like(wl)


def apply_kernel(b, u, own, own_weights, rest, rest_weights, root, root_weights, out_hbm, u_hbm, ready, out_sems, u_sem, *, accs):
    tiles = root.shape[0] // TILE
    u_copy = pltpu.make_async_copy(u, u_hbm, u_sem)
    u_copy.start()
    early = own.shape[0] // TILE
    is_root = lax.axis_index("col") == 0

    def out_copy(g):
        rows = pl.ds(pl.multiple_of(g * (WAYS * TILE), TILE), WAYS * TILE)
        return pltpu.make_async_copy(ready.at[rows, :], out_hbm.at[rows, :], out_sems.at[g])

    def product(*accs):
        for unit in range(2):
            pltpu.matmul_push_rhs(b[...], 0, unit)

        def begin(slot, t, first):
            h, l = halves(root[tile_rows(jnp.minimum(t, tiles - 1)), :])
            a = jnp.concatenate([h, l], 1)
            pltpu.matmul_acc_lhs(accs[slot], a, load_staged_rhs=0 if first else None)

        for slot in range(WAYS):
            begin(slot, slot, slot < 2)

        def part(block, weights, first):
            def group(g, carry):
                for slot in range(WAYS):
                    at = g * WAYS + slot
                    t = first + at
                    p = pltpu.matmul_pop(accs[slot])
                    prod = (p[:, 0:TILE] + p[:, TILE:]) * root_weights[pl.ds(t, 1), :]
                    base = jnp.where(is_root, 0.0, block[tile_rows(at), :] * weights[pl.ds(at, 1), :])
                    ready[tile_rows(t), :] = base + prod
                    begin(slot, t + WAYS, False)
                out_copy(first // WAYS + g).start()
                return carry

            lax.fori_loop(0, block.shape[0] // TILE // WAYS, group, 0)

        part(own, own_weights, 0)
        part(rest, rest_weights, early)
        for acc in accs:
            pltpu.matmul_pop(acc)

    pl.run_scoped(product, *accs[:WAYS])

    def finish(g, carry):
        out_copy(g).wait()
        return carry

    lax.fori_loop(0, tiles // WAYS, finish, 0)
    u_copy.wait()


def vmem():
    return pl.BlockSpec(memory_space=pltpu.VMEM)


def hbm():
    return pl.BlockSpec(memory_space=pltpu.HBM)


def numbered(send, steps):
    parts = []
    for k in steps:
        parts.append(send(k))
    return parts


def limit(mib):
    return pltpu.CompilerParams(vmem_limit_bytes=mib * 1024 * 1024)


def steps(accs, colloc_points, sources, counts, row_element, pivots):
    local_rows = colloc_points.shape[1]
    tiles = local_rows // TILE
    early = tiles // 2
    own_counts = counts.reshape(tiles)
    col = lax.axis_index("col")

    def stay(v):
        return pltpu.with_memory_space_constraint(v, pltpu.HBM)

    table = jax.ShapeDtypeStruct((PAIRS, FEATS, 2 * TILE), BF)
    aside = jax.ShapeDtypeStruct((FEATS, 2 * TILE), BF)

    def part(count):
        return jax.ShapeDtypeStruct((count * TILE, TILE), F32)

    def rows(count):
        return jax.ShapeDtypeStruct((count, TILE), F32)

    wide = pltpu.VMEM((QUAD_MAX * FEATS, TILE), F32)
    message_block = jax.ShapeDtypeStruct((8, TILE), F32)
    scalar_counts = pltpu.SMEM((tiles,), I32)
    scalar_message = pltpu.SMEM((8, TILE), F32)
    lists = [pltpu.VMEM((3, TILE, TILE), BF), pltpu.SMEM((PAIRS, tiles + 1), I32), pltpu.SMEM((PAIRS + 1,), I32)]

    message, points, elements, pivot_row = pl.pallas_call(
        pack_kernel,
        out_shape=(
            message_block,
            jax.ShapeDtypeStruct(colloc_points.shape, F32),
            jax.ShapeDtypeStruct((tiles, TILE), I32),
            jax.ShapeDtypeStruct((1, TILE), I32),
        ),
        in_specs=[hbm()] * 5,
        out_specs=(vmem(),) * 4,
        scratch_shapes=[pltpu.VMEM((1, tiles), I32), pltpu.SemaphoreType.DMA((5,))],
        compiler_params=limit(4),
        name="pack",
    )(
        stay(sources),
        stay(own_counts.reshape(1, tiles)),
        stay(colloc_points),
        stay(row_element.reshape(tiles, TILE)),
        stay(pivots.reshape(1, TILE)),
    )
    got = numbered(lambda k: lax.ppermute(message, "col", [(0, k)]), (2, 3, 1))
    y_part = jnp.where(col == 0, message, got[0] + got[1] + got[2])
    got = numbered(lambda k: lax.ppermute(y_part, "col", [(i, i + k) for i in range(4)]), (8, 12, 4))
    root_message = jnp.where(col < 4, y_part, got[0] + got[1] + got[2])
    own_sum, own_weights, lhs, own_tab, own_side, found = pl.pallas_call(
        functools.partial(own_kernel, accs=accs),
        out_shape=(part(early), rows(early), jax.ShapeDtypeStruct((local_rows, TILE), BF), table, aside, message_block),
        in_specs=[hbm()] + [vmem()] * 4,
        out_specs=(vmem(),) * 6,
        scratch_shapes=[scalar_counts, wide, pltpu.VMEM((early * TILE, TILE), F32), *lists, pltpu.SemaphoreType.DMA],
        compiler_params=limit(12),
        name="own",
    )(stay(own_counts), points, elements, pivot_row, message)
    picked = pl.pallas_call(
        pick_kernel,
        out_shape=message_block,
        in_specs=[vmem()] * 2,
        out_specs=vmem(),
        compiler_params=limit(4),
        name="pick",
    )(found, root_message)
    picked = picked + lax.ppermute(picked, "row", [(i, i ^ 1) for i in range(8)])
    got = numbered(lambda k: lax.ppermute(picked, "row", [(i, i ^ k) for i in range(8)]), (4, 2, 6))
    picked = picked + got[0] + got[1] + got[2]
    rest_sum, rest_weights, root_sum, root_weights, root_tab, root_side = pl.pallas_call(
        functools.partial(rest_kernel, accs=accs),
        out_shape=(part(tiles - early), rows(tiles - early), part(tiles), rows(tiles), table, aside),
        in_specs=[hbm()] + [vmem()] * 4,
        out_specs=(vmem(),) * 6,
        scratch_shapes=[
            scalar_counts,
            scalar_message,
            wide,
            pltpu.VMEM((tiles * TILE, TILE), F32),
            *lists,
            pltpu.SemaphoreType.DMA((2,)),
        ],
        compiler_params=limit(20),
        name="rest",
    )(stay(own_counts), lhs, root_message, own_tab, own_side)
    factors, upper_rows = pl.pallas_call(
        solve_kernel,
        out_shape=(
            jax.ShapeDtypeStruct((2 * TILE, 2 * TILE), BF),
            jax.ShapeDtypeStruct((TILE, TILE), F32),
        ),
        in_specs=[vmem()] * 5,
        out_specs=(vmem(), vmem()),
        scratch_shapes=[
            pltpu.VMEM((TILE, 2 * TILE), BF),
            pltpu.VMEM((TILE, 2 * TILE), F32),
            pltpu.VMEM((TILE, TILE), F32),
        ],
        compiler_params=limit(8),
        name="solve",
    )(picked, own_tab, own_side, root_tab, root_side)
    return pl.pallas_call(
        functools.partial(apply_kernel, accs=accs),
        out_shape=(
            jax.ShapeDtypeStruct((local_rows, TILE), F32),
            jax.ShapeDtypeStruct((TILE, TILE), F32),
        ),
        in_specs=[vmem()] * 8,
        out_specs=(hbm(), hbm()),
        scratch_shapes=[
            pltpu.VMEM((local_rows, TILE), F32),
            pltpu.SemaphoreType.DMA((tiles // WAYS,)),
            pltpu.SemaphoreType.DMA,
        ],
        compiler_params=limit(20),
        name="apply",
    )(factors, upper_rows, own_sum, own_weights, rest_sum, rest_weights, root_sum, root_weights)


def body(accs, *args):
    return steps(accs, *args)


def solution(mesh):
    placed = (P(None, "row"), P(None, "col"), P("row", "col"), P("row"), P())
    with jax.sharding.use_abstract_mesh(mesh.abstract_mesh):
        accs = [pltpu.ACC(k % 2)((TILE, 2 * TILE), F32) for k in range(JOBS)]
    return jax.shard_map(
        functools.partial(body, accs),
        mesh=mesh,
        in_specs=placed,
        out_specs=(P("row", "col"), P(None, "col")),
        check_vma=False,
    )
```
